512 devices in a mesh: gx: 16 (over z, core), gy: 32 (over x, y).
Axes of the slice: x: 4, y: 8, z: 8, core: 2. Of those that a mesh axis runs over, the one named last changes fastest.
Arguments:
- state: float32 [128, 512, 256], P('gx', 'gy'), may hold values from -4 to 4
- forcing: float32 [128, 512, 256], P('gx', 'gy'), may hold values from -24 to 24
Outputs:
- new_state: float32 [128, 512, 256], P('gx', 'gy')
The draws below stay inside these ranges and needn't reach their ends.
All inputs are finite; a program needn't handle non-finite values.
Results may differ from the reference program's by a relative error of at most 0.0003.
Values sent between devices are 32-bit elements; how exact they have to be, the bound alone decides.
A program may use at most 64 MiB of HBM per device.

```python
import math
import jax
import jax.numpy as jnp
import numpy as np
from jax import lax

SWEEPS = 6
NX = 128
NY = 512
NZ = 256


def level_of(key, shape, cuts, low, top_value):
    factor_of = 1.0
    for axis_at, blocks in cuts:
        heights = jax.random.uniform(jax.random.fold_in(jax.random.fold_in(key, 6), axis_at), (blocks,), jnp.float32, low / len(cuts), top_value / len(cuts))
        factor_of = factor_of * jnp.repeat(jnp.exp(heights), shape[axis_at] // blocks).reshape((-1,) + (1,) * (len(shape) - 1 - axis_at))
    return factor_of


def scatter_about(key, extent, deviation, reach, split=(), kind=jnp.bfloat16):
    gain = level_of(key, extent, split, -0.22, 0.18) if split else 1.0
    drawn = jax.random.normal(key, extent, jnp.float32) * deviation * gain
    return jnp.minimum(jnp.maximum(drawn, -reach), reach).astype(kind)


def setup_inputs(seed: int = 0) -> dict:
    key_list = jax.random.split(jax.random.key(seed), 3)
    state = scatter_about(key_list[0], (NX, NY, NZ), 1.0, 4.0, ((0, 16), (1, 32)), jnp.float32)
    forcing = scatter_about(key_list[1], (NX, NY, NZ), 4.0, 24.0, ((0, 16), (1, 32)), jnp.float32)
    return {"state": state, "forcing": forcing}


fine_offsets = [(0, 0, 0), (-1, 0, 0), (1, 0, 0), (0, -1, 0), (0, 1, 0), (0, 0, -1), (0, 0, 1)]
coarse_offsets = [(first, second, third) for first in (-1, 0, 1) for second in (-1, 0, 1) for third in (-1, 0, 1)]
smoothing_weight = 0.6


def tap_table():
    table = np.zeros((3, 3, 3), np.float32)
    for fine_step in range(3):
        for coarse_step in range(3):
            for place in range(3):
                spread = abs((place - 1) + (fine_step - 1) - 2 * (coarse_step - 1))
                table[fine_step, coarse_step, place] = (1.0 - abs(place - 1) / 2.0) * max(0.0, 1.0 - spread / 2.0)
    return table


def strided_views(field, axis):
    count = field.shape[axis] - 1
    return [lax.slice_in_dim(field, start, start + count - 1, 2, axis) if start == 0 else lax.slice_in_dim(field, start, count + 1 if start == 2 else count, 2, axis) for start in range(3)]


def coarse_sum(field, axis):
    views = strided_views(field, axis)
    return 0.5 * views[0] + views[1] + 0.5 * views[2]


def alternate(field, axis):
    count = field.shape[axis] - 1
    base = lax.slice_in_dim(field, 0, count, 1, axis)
    following = lax.slice_in_dim(field, 1, count + 1, 1, axis)
    paired = jnp.stack([base, 0.5 * (base + following)], axis + 1)
    shape = list(base.shape)
    shape[axis] = 2 * count
    return paired.reshape(shape)


def edge_masks(first, count, total):
    rows = first + jnp.arange(count, dtype=jnp.int32)
    return jnp.stack([((rows + step >= 0) & (rows + step < total)).astype(jnp.float32) for step in (-1, 0, 1)])


def row_flags(first, count, total):
    rows = first + jnp.arange(count, dtype=jnp.int32)
    interior_flag = ((rows >= 0) & (rows < total)).astype(jnp.float32)
    return interior_flag, (rows > 0).astype(jnp.float32), (rows < total - 1).astype(jnp.float32)


def face_weight(centre, beside):
    return 1.0 + jnp.square(0.5 * (centre + beside))


def fine_stencil(padded, row_valid, down_ok, up_ok):
    centre = padded[1:-1, 1:-1, 1:-1]
    depth = centre.shape[2]
    layers = jnp.arange(depth, dtype=jnp.int32)
    down_z = (layers > 0).astype(jnp.float32)
    up_z = (layers < depth - 1).astype(jnp.float32)
    west = face_weight(centre, padded[:-2, 1:-1, 1:-1])
    east = face_weight(centre, padded[2:, 1:-1, 1:-1])
    south = face_weight(centre, padded[1:-1, :-2, 1:-1])
    north = face_weight(centre, padded[1:-1, 2:, 1:-1])
    below = face_weight(centre, padded[1:-1, 1:-1, :-2])
    above = face_weight(centre, padded[1:-1, 1:-1, 2:])
    diagonal = west + east + south + north + below + above
    rows = row_valid[None, :, None]
    parts = [diagonal, -west, -east, -south * down_ok[None, :, None], -north * up_ok[None, :, None], -below * down_z, -above * up_z]
    return jnp.stack([part * rows for part in parts])


def apply_stencil(stack, offsets, padded):
    size_x, size_y, size_z = stack.shape[1:]
    return sum(stack[number] * padded[1 + offset[0]:1 + offset[0] + size_x, 1 + offset[1]:1 + offset[1] + size_y, 1 + offset[2]:1 + offset[2] + size_z] for number, offset in enumerate(offsets))


def galerkin(extended, offsets, row_masks, depth_masks):
    field = jnp.pad(extended, ((0, 0), (0, 0), (0, 0), (1, 0)))
    table = tap_table()
    taps_first = jnp.asarray(np.stack([table[offset[0] + 1] for offset in offsets]))
    taps_second = jnp.asarray(np.stack([table[offset[1] + 1] for offset in offsets]))
    third_stencil_taps = jnp.asarray(np.stack([table[offset[2] + 1] for offset in offsets]))
    depth_in = field.shape[3]
    depth_out = (depth_in - 1) // 2
    fine_index = jnp.arange(depth_in, dtype=jnp.int32)[:, None]
    coarse_index = jnp.arange(depth_out, dtype=jnp.int32)[None, :]
    picker_masks = jnp.stack([(fine_index - 2 * coarse_index == place).astype(jnp.float32) for place in range(3)])
    depth_lookup = jnp.einsum("dql,ljg->djqg", third_stencil_taps, picker_masks, precision=lax.Precision.HIGHEST)
    section = jnp.einsum("kxyf,kfsc->ksxyc", field, depth_lookup, precision=lax.Precision.HIGHEST)
    views = strided_views(section, 2)
    section = sum(taps_first[:, :, place][:, :, None, None, None, None] * views[place][:, None] for place in range(3))
    views = strided_views(section, 4)
    section = sum(taps_second[:, :, place][:, None, :, None, None, None, None] * views[place][:, :, None] for place in range(3))
    total = jnp.sum(section, 0)
    total = total * row_masks[None, :, None, None, :, None] * depth_masks[None, None, :, None, None, :]
    return total.reshape((27,) + total.shape[3:])


def pad_global(field):
    wrapped = jnp.concatenate([field[-1:], field, field[:1]], 0)
    return jnp.pad(wrapped, ((0, 0), (1, 1), (1, 1)))


def lower_global(stack):
    extended = jnp.concatenate([stack[:, -1:], stack], 1)
    return jnp.pad(extended, ((0, 0), (0, 0), (1, 0), (0, 0)))


def restrict_global(residual):
    extended = lower_global(residual[None])[0]
    extended = jnp.pad(extended, ((0, 0), (0, 0), (1, 0)))
    return coarse_sum(coarse_sum(coarse_sum(extended, 0), 1), 2)


def prolong_global(coarser_grid):
    finer = alternate(jnp.concatenate([coarser_grid, coarser_grid[:1]], 0), 0)
    finer = alternate(jnp.pad(finer, ((0, 0), (0, 1), (0, 0))), 1)
    return alternate(jnp.pad(finer, ((0, 0), (0, 0), (0, 1))), 2)


def galerkin_blocks(extended, offsets):
    coarse_x = (extended.shape[1] - 1) // 2
    coarse_y = (extended.shape[2] - 1) // 2
    coarse_z = extended.shape[3] // 2
    row_masks = edge_masks(0, coarse_y, coarse_y)
    depth_masks = edge_masks(0, coarse_z, coarse_z)
    block = math.gcd(coarse_x, 8)
    starts = jnp.arange(coarse_x // block, dtype=jnp.int32) * (2 * block)

    def single_block(start):
        piece = lax.dynamic_slice_in_dim(extended, start, 2 * block + 1, 1)
        return galerkin(piece, offsets, row_masks, depth_masks)

    pieces = lax.map(single_block, starts)
    return jnp.moveaxis(pieces, 0, 1).reshape((27, coarse_x, coarse_y, coarse_z))


def cycle(stacks, level, source):
    stack = stacks[level]
    offsets = fine_offsets if level == 0 else coarse_offsets
    centre = stack[offsets.index((0, 0, 0))]
    correction = smoothing_weight * source / centre
    if level == len(stacks) - 1:
        for sweep in range(SWEEPS - 1):
            correction = correction + smoothing_weight * (source - apply_stencil(stack, offsets, pad_global(correction))) / centre
        return correction
    residual = source - apply_stencil(stack, offsets, pad_global(correction))
    correction = correction + prolong_global(cycle(stacks, level + 1, restrict_global(residual)))
    return correction + smoothing_weight * (source - apply_stencil(stack, offsets, pad_global(correction))) / centre


def reference(state, forcing):
    size_y = state.shape[1]
    padded = pad_global(state)
    row_valid, down_ok, up_ok = row_flags(0, size_y, size_y)
    fine = fine_stencil(padded, row_valid, down_ok, up_ok)
    newton = forcing - apply_stencil(fine, fine_offsets, padded)
    stacks = [fine]
    offsets = fine_offsets
    for level in range(3):
        coarser_grid = galerkin_blocks(lower_global(stacks[-1]), offsets)
        stacks.append(coarser_grid)
        offsets = coarse_offsets
    return state + cycle(stacks, 0, newton)
```

```python
import jax
import jax.numpy as jnp
from jax import lax
from jax.experimental import pallas as pl
from jax.experimental.pallas import tpu as pltpu
from jax.sharding import PartitionSpec as P

WEIGHT = 0.6
MESH = pl.DeviceIdType.MESH
F32 = jnp.float32

AROUND = [(a, b) for a in (-1, 0, 1) for b in (-1, 0, 1) if (a, b) != (0, 0)]
WIDE = [(a, b) for a in range(-3, 5) for b in range(-2, 3) if (a, b) != (0, 0)]
GREETED = [(a, b) for a in range(-4, 5) for b in range(-2, 3) if (a, b) != (0, 0)]
FORWARD = [(0, 0, 0), (0, 0, 1), (1, 0, -1), (1, 0, 0), (1, 0, 1)] + [
    (a, 1, c) for a in (-1, 0, 1) for c in (-1, 0, 1)
]
ALL = [(a, b, c) for b in (-1, 0, 1) for a in (-1, 0, 1) for c in (-1, 0, 1)]
BACKWARD = [o for o in ALL if o not in FORWARD]


def iota(shape, dim):
    return lax.broadcasted_iota(jnp.int32, shape, dim)


def xsh(f, by):
    if by == 0:
        return f
    return pltpu.roll(f, 7 if by == 1 else 1, f.ndim - 2)


def zsh(f, by, d):
    if by == 0:
        return f
    lane = iota(f.shape, f.ndim - 1)
    if by == 1:
        return jnp.where(lane < 128 - d, pltpu.roll(f, 128 - d, f.ndim - 1), 0.0)
    return jnp.where(lane >= d, pltpu.roll(f, d, f.ndim - 1), 0.0)


def face(a, b):
    return 1.0 + jnp.square(0.5 * (a + b))


def kernel_body(n, m, x_ref, f_ref, o_ref, s):
    gx, gy = lax.axis_index("gx"), lax.axis_index("gy")

    def device(a, b):
        return (lax.rem(gx + a + n, n), lax.rem(gy + b + m, m))

    started = []

    def send(src, dst, number, a, b):
        copy = pltpu.make_async_remote_copy(
            src_ref=src,
            dst_ref=dst,
            send_sem=s.ssem.at[number],
            recv_sem=s.rsem.at[number],
            device_id=device(a, b),
            device_id_type=MESH,
        )
        copy.start()
        started.append(copy)
        return copy

    def inside(first, shape, width):
        rows = gy * width + first + iota(shape, 0)
        return (rows >= 0) & (rows < m * width)

    barrier = pltpu.get_barrier_semaphore()
    for a, b in GREETED:
        pl.semaphore_signal(barrier, inc=1, device_id=device(a, b), device_id_type=MESH)

    lane = iota((16, 128), 1)
    low = lane < 64
    take_a = jnp.where(low, 2 * lane, 2 * lane - 127)
    take_b = jnp.where(low, 2 * lane + 1, 2 * lane - 128)
    for ref, split in ((x_ref, s.split_u), (f_ref, s.split_f)):
        for x in range(8):
            va = jnp.take_along_axis(ref[x, :, 0:128], take_a, axis=1, mode="promise_in_bounds")
            vb = jnp.take_along_axis(ref[x, :, 128:256], take_b, axis=1, mode="promise_in_bounds")
            place = ((x % 2) * 4 + x // 2) * 16
            split[0, place : place + 16, :] = jnp.where(low, va, vb)
            split[1, place : place + 16, :] = pltpu.roll(jnp.where(low, vb, va), 64, 1)
    for z in range(2):
        for y in range(16):
            u = s.split_u[z, pl.ds(y, 8, stride=16), :]
            f = s.split_f[z, pl.ds(y, 8, stride=16), :]
            s.cu[z, 4 + y] = u
            s.cf[z, 4 + y] = f
    for side, at in ((0, 2), (1, 0)):
        for z in range(2):
            s.px[side, z, :, 0:2, :] = s.cu[z, 4:20, at : at + 2, :]
            s.px[side, z, :, 2:4, :] = s.cu[z, 4:20, at + 4 : at + 6, :]
            s.px[side, z, :, 4:6, :] = s.cf[z, 4:20, at : at + 2, :]
            s.px[side, z, :, 6:8, :] = s.cf[z, 4:20, at + 4 : at + 6, :]
    pl.semaphore_wait(barrier, len(GREETED))

    source_rows = {-1: pl.ds(0, 4), 0: pl.ds(0, 16), 1: pl.ds(12, 4)}
    target_rows = {-1: pl.ds(20, 4), 0: pl.ds(4, 16), 1: pl.ds(0, 4)}
    round1 = []
    number = 0
    for a in (1, -1):
        side = 0 if a == 1 else 1
        for b in (0, 1, -1):
            round1.append(
                send(
                    s.px.at[side, :, source_rows[b]],
                    s.rx.at[side, :, target_rows[b]],
                    number,
                    a,
                    b,
                )
            )
            number += 1
    for b in (1, -1):
        here = pl.ds(16, 4) if b == 1 else pl.ds(4, 4)
        for ref in (s.cu, s.cf):
            round1.append(send(ref.at[:, here], ref.at[:, target_rows[b]], number, 0, b))
            number += 1
    for copy in round1:
        copy.wait_recv()

    def assemble(i, carry):
        at = pl.ds(4 * i, 4)
        keep = inside(4 * i - 4, (4, 8, 128), 16)
        sub = iota((4, 8, 128), 1)
        for z in range(2):
            lo, mid_u, mid_f, hi = s.rx[0, z, at], s.cu[z, at], s.cf[z, at], s.rx[1, z, at]
            for x in range(2):
                for base, mid, ref in ((0, mid_u, s.u), (4, mid_f, s.f)):
                    a = base + 2 * x
                    left = pltpu.roll(lo, (8 - a) % 8, 1) if a else lo
                    here = pltpu.roll(mid, (2 - 4 * x) % 8, 1)
                    right = pltpu.roll(hi, (6 - a) % 8, 1) if (6 - a) % 8 else hi
                    value = jnp.where(sub < 2, left, jnp.where(sub < 6, here, right))
                    ref[2 * z + x, at] = jnp.where(keep, value, 0.0)
        return carry

    lax.fori_loop(0, 6, assemble, 0)
    s.u[:, 24:26] = jnp.zeros((4, 2, 8, 128), F32)

    def faces(i, carry):
        at, above = pl.ds(2 * i, 2), pl.ds(2 * i + 1, 2)
        u = [s.u[p, at] for p in range(4)]
        un = [s.u[p, above] for p in range(4)]
        keep = inside(2 * i - 4, (2, 8, 128), 16)
        first = iota((2, 8, 128), 2) == 0
        sx, sz, szd, ky = [], [], [], []
        for z in range(2):
            ka, kb = face(u[2 * z], u[2 * z + 1]), face(u[2 * z + 1], xsh(u[2 * z], 1))
            s.kx[z, at], s.kx[2 + z, at] = ka, kb
            sx.append(0.25 * (ka + kb))
        for x in range(2):
            ka, kb = face(u[x], u[2 + x]), face(u[2 + x], zsh(u[x], 1, 1))
            s.kz[x, at], s.kz[2 + x, at] = ka, kb
            sz.append(0.25 * (ka + kb))
            szd.append(jnp.where(first, face(u[x], 0.0), zsh(sz[x], -1, 1)))
        for p in range(4):
            ky.append(face(u[p], un[p]))
            s.ky[p, at] = ky[p]

        def mx(f0, f1):
            return f0 + 0.25 * (f1 + xsh(f1, -1)), 0.25 * f1

        def mz(f0, f1):
            return f0 + 0.25 * (f1 + zsh(f1, -1, 1)), 0.25 * f1

        sx0, sxp = mz(sx[0], sx[1])
        t0, tp = mx(sz[0], sz[1])
        d0, dp = mx(szd[0], szd[1])
        for k, value in enumerate((sx0, sxp, t0, tp, t0 + d0, tp + dp)):
            s.g[k, at] = jnp.where(keep, value, 0.0)
        h0, hp = mx(ky[0], ky[1])
        j0, jp = mx(ky[2], ky[3])
        h00, h0p = mz(h0, j0)
        hp0, hpp = mz(hp, jp)
        for k, value in enumerate((h00, h0p, hp0, hpp)):
            s.h[k, at] = value
        return carry

    lax.fori_loop(0, 12, faces, 0)

    def beside(ref, row, k):
        at = pl.ds(row, k)
        v = [ref[p, at] for p in range(4)]
        out = []
        for z in range(2):
            for x in range(2):
                p = 2 * z + x
                ka, kb = s.kx[z, at], s.kx[2 + z, at]
                w = v[2 * z + 1 - x]
                if x == 0:
                    total = ka * w + xsh(kb * w, -1)
                else:
                    total = ka * w + kb * xsh(w, 1)
                ka, kb = s.kz[x, at], s.kz[2 + x, at]
                w = v[2 * (1 - z) + x]
                if z == 0:
                    total += ka * w + zsh(kb * w, -1, 1)
                else:
                    total += ka * w + kb * zsh(w, 1, 1)
                total += s.ky[p, at] * ref[p, pl.ds(row + 1, k)]
                total += s.ky[p, pl.ds(row - 1, k)] * ref[p, pl.ds(row - 1, k)]
                out.append(total)
        return v, out

    def smooth0(i, carry):
        row = 2 + 2 * i
        at = pl.ds(row, 2)
        keep = inside(row - 4, (2, 8, 128), 16)
        first = iota((2, 8, 128), 2) == 0
        v, total = beside(s.u, row, 2)
        for z in range(2):
            for x in range(2):
                p = 2 * z + x
                ka, kb = s.kx[z, at], s.kx[2 + z, at]
                diag = ka + (xsh(kb, -1) if x == 0 else kb)
                ka, kb = s.kz[x, at], s.kz[2 + x, at]
                if z == 0:
                    diag += ka + jnp.where(first, face(v[p], 0.0), zsh(kb, -1, 1))
                else:
                    diag += ka + kb
                diag += s.ky[p, at] + s.ky[p, pl.ds(row - 1, 2)]
                newton = s.f[p, at] - (diag * v[p] - total[p])
                weight = WEIGHT / diag
                s.f[p, at] = newton
                s.d0[p, at] = diag
                s.w0[p, at] = weight
                s.e0[p, at] = jnp.where(keep, weight * newton, 0.0)
        return carry

    lax.fori_loop(0, 10, smooth0, 0)

    def residual0(i, carry):
        row = 3 + 2 * i
        at = pl.ds(row, 2)
        keep = inside(row - 4, (2, 8, 128), 16)
        v, total = beside(s.e0, row, 2)
        r = [s.f[p, at] - (s.d0[p, at] * v[p] - total[p]) for p in range(4)]
        r = [r[x] + 0.5 * (r[2 + x] + zsh(r[2 + x], -1, 1)) for x in range(2)]
        s.r0[at] = jnp.where(keep, r[0] + 0.5 * (r[1] + xsh(r[1], -1)), 0.0)
        return carry

    lax.fori_loop(0, 9, residual0, 0)

    def level1(i, only_up):
        base = 2 * i
        edge = (gy == 0) & (i == 2)
        keep = inside(i - 2, (1, 8, 128), 8)[0]

        def v_of(q, row):
            return 0.25 * (s.h[q, row] + s.h[q, row + 1])

        v = [v_of(q, base) for q in range(4)]
        up = [0.25 * s.g[k, base + 1] for k in range(6)]
        sx0, sxp, t0, tp, p0, pp = up
        arrays = {
            (0, 0): sx0 + xsh(sx0, -1) + p0 - v[0],
            (0, 1): sxp + xsh(sxp, -1) - t0 - v[1],
            (1, 0): pp - sx0 - v[2],
            (1, 1): -sxp - tp - v[3],
        }
        fill(9, i, arrays, keep)
        if only_up:
            return
        vd = [jnp.where(edge, s.h[q, base - 1], v_of(q, base - 2)) for q in range(4)]
        both = [v[q] + vd[q] for q in range(4)]
        sx0, sxp, t0, tp, p0, pp = [
            s.g[k, base] + up[k] + 0.25 * s.g[k, base - 1] for k in range(6)
        ]
        arrays = {
            (0, 0): sx0 + xsh(sx0, -1) + p0 + both[0],
            (0, 1): sxp + xsh(sxp, -1) - t0 + both[1],
            (1, 0): pp - sx0 + both[2],
            (1, 1): both[3] - sxp - tp,
        }
        fill(0, i, arrays, keep)
        s.w1[i] = jnp.where(keep, WEIGHT / arrays[(0, 0)], 0.0)

    def fill(first, i, arrays, keep):
        for key in arrays:
            arrays[key] = jnp.where(keep, arrays[key], 0.0)
        for a in (-1, 0, 1):
            for c in (-1, 0, 1):
                value = zsh(arrays[(abs(a), abs(c))], min(c, 0), 1)
                s.a1[first + 3 * (a + 1) + c + 1, i] = xsh(value, min(a, 0))

    def coefficient1(o, row, k):
        a, b, c = o
        at = 3 * (a + 1) + c + 1
        if b == 0:
            return s.a1[at, pl.ds(row, k)]
        return s.a1[9 + at, pl.ds(row if b == 1 else row - 1, k)]

    level1(0, True)

    def level1_step(i, carry):
        level1(i, False)
        return carry

    lax.fori_loop(1, 11, level1_step, 0)

    sub = iota((8, 128), 0)

    def start1(y, carry):
        row = 4 + 2 * y
        b1 = s.r0[row] + 0.5 * (s.r0[row - 1] + s.r0[row + 1])
        e1 = s.w1[y + 2] * b1
        s.re1[1, y + 2] = jnp.where(sub < 4, pltpu.roll(e1, 6, 0), pltpu.roll(b1, 2, 0))
        return carry

    lax.fori_loop(0, 8, start1, 0)

    mine = {-1: pl.ds(2, 2), 0: pl.ds(2, 8), 1: pl.ds(8, 2)}
    theirs = {-1: pl.ds(10, 2), 0: pl.ds(2, 8), 1: pl.ds(0, 2)}
    round2 = []
    for a, b in AROUND:
        round2.append(send(s.re1.at[1, mine[b]], s.re1.at[1 - a, theirs[b]], number, a, b))
        number += 1

    def coarsen(coefficient, row, d, store):
        def get(o, r):
            return coefficient(o, r, 1)[0]

        y0, y1 = {}, {}
        for a in (-1, 0, 1):
            for c in (-1, 0, 1):
                zero_up = 0.25 * get((a, 0, c), row + 1)
                plus = get((a, 1, c), row)
                y0[a, c] = (
                    get((a, 0, c), row)
                    + zero_up
                    + 0.25 * get((a, 0, c), row - 1)
                    + 0.5
                    * (
                        get((a, -1, c), row)
                        + get((a, -1, c), row + 1)
                        + plus
                        + get((a, 1, c), row - 1)
                    )
                )
                y1[a, c] = 0.5 * (plus + get((a, 1, c), row + 1)) + zero_up

        def three(lo, mid, hi, shift, want):
            out = {}
            q = 0.25 * mid
            lo, hi = 0.5 * lo, 0.5 * hi
            if 0 in want:
                out[0] = mid + lo + hi + shift(q + lo, 1) + shift(q + hi, -1)
            if 1 in want:
                out[1] = hi + shift(q + hi, 1)
            if -1 in want:
                out[-1] = lo + shift(q + lo, -1)
            return out

        def by_z(f, by):
            return zsh(f, by, d)

        for b, table in ((0, y0), (1, y1)):
            xs = {}
            for c in (-1, 0, 1):
                want = (0, 1) if b == 0 else (-1, 0, 1)
                got = three(table[-1, c], table[0, c], table[1, c], xsh, want)
                for a in got:
                    xs[a, c] = got[a]
            for a in (0, 1) if b == 0 else (-1, 0, 1):
                want = (0, 1) if (a, b) == (0, 0) else (-1, 0, 1)
                got = three(xs[a, -1], xs[a, 0], xs[a, 1], by_z, want)
                for c in got:
                    store(FORWARD.index((a, b, c)), got[c])

    def coarsen1(y, carry):
        def store(k, value):
            s.ra2[1, y + 2, k // 4, 2 * (k % 4) : 2 * (k % 4) + 1, :] = value[2:3]
            s.ra2[1, y + 2, k // 4, 2 * (k % 4) + 1 : 2 * (k % 4) + 2, :] = value[4:5]
            if k == 0:
                s.w2own[y] = WEIGHT / value

        coarsen(coefficient1, 2 * y + 2, 1, store)
        return carry

    lax.fori_loop(0, 4, coarsen1, 0)
    mine = {-1: pl.ds(2, 2), 0: pl.ds(2, 4), 1: pl.ds(4, 2)}
    theirs = {-1: pl.ds(6, 2), 0: pl.ds(2, 4), 1: pl.ds(0, 2)}
    round2a = []
    for a, b in AROUND:
        round2a.append(send(s.ra2.at[1, mine[b]], s.ra2.at[1 - a, theirs[b]], number, a, b))
        number += 1
    for b in (-1, 0, 1):
        round2a.append(send(s.ra2.at[1, mine[b], 1], s.ra2.at[3, theirs[b], 1], number, -2, b))
        number += 1

    for copy in round2:
        copy.wait_recv()

    def unpack1(i, carry):
        at = pl.ds(2 * i, 2)
        keep = inside(2 * i - 2, (2, 8, 128), 8)
        sub = iota((2, 8, 128), 1)
        lo, mid, hi = s.re1[0, at], s.re1[1, at], s.re1[2, at]
        e = jnp.where(
            sub < 2,
            pltpu.roll(lo, 6, 1),
            jnp.where(sub < 6, pltpu.roll(mid, 2, 1), pltpu.roll(hi, 6, 1)),
        )
        b = jnp.where(
            sub < 2,
            pltpu.roll(lo, 2, 1),
            jnp.where(sub < 6, pltpu.roll(mid, 6, 1), pltpu.roll(hi, 2, 1)),
        )
        s.e1[at] = jnp.where(keep, e, 0.0)
        s.b1[at] = jnp.where(keep, b, 0.0)
        return carry

    lax.fori_loop(0, 6, unpack1, 0)

    def apply(coefficient, ref, row, k, d):
        total = None
        for b in (-1, 0, 1):
            e = ref[pl.ds(row + b, k)]
            for c in (-1, 0, 1):
                ez = zsh(e, c, d)
                for a in (-1, 0, 1):
                    term = coefficient((a, b, c), row, k) * xsh(ez, a)
                    total = term if total is None else total + term
        return total

    def gather_zx(r, d):
        r = r + 0.5 * (zsh(r, -1, d) + zsh(r, 1, d))
        return r + 0.5 * (xsh(r, -1) + xsh(r, 1))

    def residual1(i, carry):
        row = 1 + i
        keep = inside(row - 2, (1, 8, 128), 8)
        r = s.b1[pl.ds(row, 1)] - apply(coefficient1, s.e1, row, 1, 1)
        s.r1[pl.ds(row, 1)] = jnp.where(keep, gather_zx(r, 1), 0.0)
        return carry

    lax.fori_loop(0, 9, residual1, 0)

    def start2(y, carry):
        row = 2 * y + 2
        b2 = s.r1[row] + 0.5 * (s.r1[row - 1] + s.r1[row + 1])
        e2 = s.w2own[y] * b2
        s.re2[1, y + 2, 0:1, :] = e2[2:3]
        s.re2[1, y + 2, 1:2, :] = e2[4:5]
        s.re2[1, y + 2, 2:3, :] = b2[2:3]
        s.re2[1, y + 2, 3:4, :] = b2[4:5]
        return carry

    lax.fori_loop(0, 4, start2, 0)

    mine = {-1: pl.ds(2, 3), 0: pl.ds(2, 4), 1: pl.ds(4, 2)}
    theirs = {-1: pl.ds(6, 3), 0: pl.ds(2, 4), 1: pl.ds(0, 2)}
    round3 = []
    for a, b in AROUND + [(-2, -1), (-2, 0), (-2, 1)]:
        round3.append(send(s.re2.at[1, mine[b]], s.re2.at[1 - a, theirs[b]], number, a, b))
        number += 1

    for copy in round2a:
        copy.wait_recv()

    def unpack_a2(i, carry):
        at = pl.ds(2 * i, 2)
        keep = inside(2 * i - 2, (2, 8, 128), 4)
        sub = iota((2, 8, 128), 1)
        for t in range(4):
            lo, mid, hi = s.ra2[0, at, t], s.ra2[1, at, t], s.ra2[2, at, t]
            for j in range(4):
                k = 4 * t + j
                if k >= 14:
                    continue

                def rolled(v, to):
                    by = (to - 2 * j) % 8
                    return pltpu.roll(v, by, 1) if by else v

                value = jnp.where(sub < 4, rolled(mid, 2), rolled(hi, 4))
                if t == 1:
                    value = jnp.where(sub < 6, value, rolled(s.ra2[3, at, 1], 6))
                value = jnp.where(sub < 2, rolled(lo, 0), value)
                value = jnp.where(keep, value, 0.0)
                s.a2[k, at] = value
                if k == 0:
                    s.w2[at] = jnp.where(keep, WEIGHT / value, 0.0)
        return carry

    lax.fori_loop(0, 4, unpack_a2, 0)

    def expand(ref, back, row, d):
        for k, (a, b, c) in enumerate(BACKWARD):
            value = ref[FORWARD.index((-a, -b, -c)), pl.ds(row + b, 1)]
            back[k, pl.ds(row, 1)] = xsh(zsh(value, c, d), a)

    def reader(ref, back):
        def coefficient(o, row, k):
            if o in FORWARD:
                return ref[FORWARD.index(o), pl.ds(row, k)]
            return back[BACKWARD.index(o), pl.ds(row, k)]

        return coefficient

    def expand2(i, carry):
        expand(s.a2, s.a2b, i, 2)
        return carry

    lax.fori_loop(1, 8, expand2, 0)
    coefficient2 = reader(s.a2, s.a2b)

    def coarsen2(y, carry):
        def store(k, value):
            s.a3own[k, y] = value

        coarsen(coefficient2, 2 * y + 2, 2, store)
        return carry

    lax.fori_loop(0, 2, coarsen2, 0)
    lane = iota((8, 128), 1)
    own = pl.ds(24, 8)
    for y in range(2):
        for q in range(4):
            value = s.a3own[4 * q, y]
            for j in range(1, 4):
                if 4 * q + j < 14:
                    other = pltpu.roll(s.a3own[4 * q + j, y], j, 1)
                    value = jnp.where(lane % 4 == j, other, value)
            s.ra3[2, 24 + 4 * y + q : 25 + 4 * y + q, :] = value[2:3]

    def send_wide(ref, number):
        copies = []
        for a, b in WIDE:
            copies.append(send(ref.at[2, own], ref.at[2 + b, pl.ds(8 * (a + 3), 8)], number, -a, -b))
            number += 1
        return copies, number

    round3a, number = send_wide(s.ra3, number)

    for copy in round3:
        copy.wait_recv()
    for k in range(4):
        at = slice(2 * k, 2 * k + 2)
        keep = inside(-2, (9, 2, 128), 4)
        s.e2[0:9, at, :] = jnp.where(keep, s.re2[k, 0:9, 0:2, :], 0.0)
        s.b2[0:9, at, :] = jnp.where(keep, s.re2[k, 0:9, 2:4, :], 0.0)

    def residual2(i, carry):
        row = 1 + i
        keep = inside(row - 2, (1, 8, 128), 4)
        r = s.b2[pl.ds(row, 1)] - apply(coefficient2, s.e2, row, 1, 2)
        s.r2[pl.ds(row, 1)] = jnp.where(keep, gather_zx(r, 2), 0.0)
        return carry

    lax.fori_loop(0, 5, residual2, 0)
    for y in range(2):
        row = 2 * y + 2
        b3 = s.r2[row] + 0.5 * (s.r2[row - 1] + s.r2[row + 1])
        e3 = WEIGHT * b3 / s.a3own[0, y]
        s.rb3[2, 24 + y : 25 + y, :] = b3[2:3]
        s.rb3[2, 26 + y : 27 + y, :] = e3[2:3]

    round4, number = send_wide(s.rb3, number)
    for copy in round3a:
        copy.wait_recv()

    for dy in range(5):
        for y in range(2):
            row = 2 * dy + y
            keep = inside(row - 4, (1, 8, 128), 2)[0]
            for q in range(4):
                value = jnp.where(keep, s.ra3[dy, pl.ds(4 * y + q, 8, stride=8), :], 0.0)
                for j in range(4):
                    if 4 * q + j < 14:
                        s.a3[4 * q + j, row] = pltpu.roll(value, 128 - j, 1) if j else value
            s.w3[row] = jnp.where(keep, WEIGHT / s.a3[0, row], 0.0)

    def expand3(i, carry):
        expand(s.a3, s.a3b, i, 4)
        return carry

    lax.fori_loop(2, 9, expand3, 0)
    coefficient3 = reader(s.a3, s.a3b)

    for copy in round4:
        copy.wait_recv()
    for dy in range(5):
        for y in range(2):
            row = 2 * dy + y
            keep = inside(row - 4, (1, 8, 128), 2)[0]
            b3 = s.rb3[dy, pl.ds(y, 8, stride=8), :]
            e3 = s.rb3[dy, pl.ds(2 + y, 8, stride=8), :]
            s.b3[row] = jnp.where(keep, b3, 0.0)
            s.e3[0, row] = jnp.where(keep, e3, 0.0)

    def sweep(source, target, low, high):
        def step(row, carry):
            at = pl.ds(row, 1)
            old, new = s.e3.at[source], s.e3.at[target]
            r = s.b3[at] - apply(coefficient3, old, row, 1, 4)
            new[at] = old[at] + s.w3[at] * r
            return carry

        lax.fori_loop(low + 4, high + 5, step, 0)

    sweep(0, 1, -2, 3)
    sweep(1, 0, -1, 2)
    sweep(0, 1, 0, 1)
    for y in range(2):
        s.re3[2, 24 + y : 25 + y, :] = s.e3[1, 4 + y, 3:4, :]

    round5, number = send_wide(s.re3, number)
    for copy in round5:
        copy.wait_recv()
    for dy in range(5):
        for y in range(2):
            row = 2 * dy + y
            keep = inside(row - 4, (1, 8, 128), 2)[0]
            e3 = s.re3[dy, pl.ds(y, 8, stride=8), :]
            s.e3[0, row] = jnp.where(keep, e3, 0.0)
    sweep(0, 1, -2, 4)
    sweep(1, 0, -1, 3)

    def spread(c, first, d, place):
        rows = c.shape[0]
        half = 0.5 * (c + xsh(c, 1))
        for k in range(4):
            place[0:rows, 2 * k : 2 * k + 1, :] = c[:, first + k : first + k + 1]
            place[0:rows, 2 * k + 1 : 2 * k + 2, :] = half[:, first + k : first + k + 1]
        value = place[0:rows]
        coarse = iota(value.shape, 2) % (2 * d) == 0
        place[0:rows] = jnp.where(coarse, value, 0.5 * (zsh(value, -1, d) + zsh(value, 1, d)))

    def add_rows(place, rows, target, width):
        for i in range(rows):
            value = place[i // 2]
            if i % 2:
                value = 0.5 * (value + place[i // 2 + 1])
            keep = inside(i - 2, (1, 8, 128), width)[0]
            target[i] = target[i] + jnp.where(keep, value, 0.0)

    spread(s.e3[0, 3:8], 2, 2, s.place)
    add_rows(s.place, 9, s.e2, 4)

    def post2(row, carry):
        at = pl.ds(row, 1)
        r = s.b2[at] - apply(coefficient2, s.e2, row, 1, 2)
        s.x2[at] = s.e2[at] + s.w2[at] * r
        return carry

    lax.fori_loop(1, 8, post2, 0)
    spread(s.x2[1:8], 1, 1, s.place)
    add_rows(s.place, 12, s.e1, 8)

    def post1(i, carry):
        row = 1 + i
        at = pl.ds(row, 1)
        r = s.b1[at] - apply(coefficient1, s.e1, row, 1, 1)
        s.x1[at] = s.e1[at] + s.w1[at] * r
        return carry

    lax.fori_loop(0, 10, post1, 0)
    s.x1[11] = jnp.zeros((8, 128), F32)

    def prolong0(i, carry):
        c = s.x1[i]
        for step in range(2):
            row = 2 * i + step
            keep = inside(row - 4, (1, 8, 128), 16)[0]
            if step:
                c = 0.5 * (c + s.x1[i + 1])
            cz = 0.5 * (c + zsh(c, 1, 1))
            values = (c, 0.5 * (c + xsh(c, 1)), cz, 0.5 * (cz + xsh(cz, 1)))
            for p in range(4):
                s.e0[p, row] = s.e0[p, row] + jnp.where(keep, values[p], 0.0)
        return carry

    lax.fori_loop(1, 11, prolong0, 0)

    def finish(i, carry):
        row = 4 + 2 * i
        at = pl.ds(row, 2)
        v, total = beside(s.e0, row, 2)
        sub = iota((2, 8, 128), 1)
        for z in range(2):
            done = []
            for x in range(2):
                p = 2 * z + x
                r = s.f[p, at] - (s.d0[p, at] * v[p] - total[p])
                value = s.u[p, at] + (v[p] + s.w0[p, at] * r)
                done.append(pltpu.roll(value, 6 if x == 0 else 2, 1))
            both = jnp.where(sub < 4, done[0], done[1])
            for k in range(2):
                s.co[z, pl.ds(pl.multiple_of(16 * i + 8 * k, 8), 8), :] = both[k]
        return carry

    lax.fori_loop(0, 8, finish, 0)

    lane = iota((16, 128), 1)
    low = lane < 64
    take = jnp.where(lane % 2 == 0, lane // 2, 64 + lane // 2)
    for x in range(8):
        place = (x % 2) * 4 + x // 2
        even = s.co[0, pl.ds(place, 16, stride=8), :]
        odd = pltpu.roll(s.co[1, pl.ds(place, 16, stride=8), :], 64, 1)
        va, vb = jnp.where(low, even, odd), pltpu.roll(jnp.where(low, odd, even), 64, 1)
        o_ref[x, :, 0:128] = jnp.take_along_axis(va, take, axis=1, mode="promise_in_bounds")
        o_ref[x, :, 128:256] = jnp.take_along_axis(vb, take, axis=1, mode="promise_in_bounds")
    for copy in started:
        copy.wait_send()


COPIES = 10 + 8 + 11 + 11 + 3 * len(WIDE)
TILE = (8, 128)
SHAPES = {
    "split_u": (2, 128, 128),
    "split_f": (2, 128, 128),
    "co": (2, 128, 128),
    "cu": (2, 24) + TILE,
    "cf": (2, 24) + TILE,
    "px": (2, 2, 16) + TILE,
    "rx": (2, 2, 24) + TILE,
    "u": (4, 26) + TILE,
    "f": (4, 26) + TILE,
    "kx": (4, 24) + TILE,
    "kz": (4, 24) + TILE,
    "ky": (4, 24) + TILE,
    "g": (6, 24) + TILE,
    "h": (4, 24) + TILE,
    "d0": (4, 24) + TILE,
    "w0": (4, 24) + TILE,
    "e0": (4, 26) + TILE,
    "r0": (24,) + TILE,
    "a1": (18, 12) + TILE,
    "w1": (12,) + TILE,
    "re1": (3, 12) + TILE,
    "e1": (12,) + TILE,
    "b1": (12,) + TILE,
    "x1": (12,) + TILE,
    "r1": (12,) + TILE,
    "ra2": (4, 8, 4) + TILE,
    "w2own": (4,) + TILE,
    "a2": (14, 8) + TILE,
    "a2b": (13, 8) + TILE,
    "w2": (8,) + TILE,
    "re2": (4, 9) + TILE,
    "e2": (9,) + TILE,
    "b2": (9,) + TILE,
    "x2": (9,) + TILE,
    "r2": (9,) + TILE,
    "a3own": (14, 2) + TILE,
    "ra3": (5, 64, 128),
    "rb3": (5, 64, 128),
    "re3": (5, 64, 128),
    "a3": (14, 10) + TILE,
    "a3b": (13, 10) + TILE,
    "w3": (10,) + TILE,
    "b3": (10,) + TILE,
    "e3": (2, 10) + TILE,
    "place": (8,) + TILE,
}


class Scratch:
    pass


def on_device(n, m, state, forcing):
    names = list(SHAPES)

    def body(x_ref, f_ref, o_ref, *scratch):
        s = Scratch()
        for name, ref in zip(names, scratch):
            setattr(s, name, ref)
        s.ssem, s.rsem = scratch[len(names) :]
        kernel_body(n, m, x_ref, f_ref, o_ref, s)

    return pl.pallas_call(
        body,
        out_shape=jax.ShapeDtypeStruct(state.shape, F32),
        in_specs=[pl.BlockSpec(memory_space=pltpu.VMEM)] * 2,
        out_specs=pl.BlockSpec(memory_space=pltpu.VMEM),
        scratch_shapes=[pltpu.VMEM(shape, F32) for shape in SHAPES.values()]
        + [pltpu.SemaphoreType.DMA((COPIES,))] * 2,
        compiler_params=pltpu.CompilerParams(
            collective_id=0, has_side_effects=True, vmem_limit_bytes=48 << 20
        ),
    )(state, forcing)


def solution(mesh):
    n, m = mesh.shape["gx"], mesh.shape["gy"]
    return jax.shard_map(
        lambda state, forcing: on_device(n, m, state, forcing),
        mesh=mesh,
        in_specs=(P("gx", "gy", None), P("gx", "gy", None)),
        out_specs=P("gx", "gy", None),
        check_vma=False,
    )
```

```python
import jax
import jax.numpy as jnp
from jax import lax
from jax.experimental import pallas as pl
from jax.experimental.pallas import tpu as pltpu
from jax.sharding import PartitionSpec as P

WEIGHT = 0.6
MESH = pl.DeviceIdType.MESH
F32 = jnp.float32

AROUND = [(a, b) for a in (-1, 0, 1) for b in (-1, 0, 1) if (a, b) != (0, 0)]
GREETED = AROUND + [(2, 0)]
WIDE = [(a, b) for a in range(-3, 5) for b in range(-2, 3) if (a, b) != (0, 0)]
ROUND1 = [(1, 1), (1, -1), (-1, 1), (-1, -1), (0, 1), (0, -1), (1, 0), (-1, 0)]
FORWARD = [(0, 0, 0), (0, 0, 1), (1, 0, -1), (1, 0, 0), (1, 0, 1)] + [
    (a, 1, c) for a in (-1, 0, 1) for c in (-1, 0, 1)
]
ALL = [(a, b, c) for b in (-1, 0, 1) for a in (-1, 0, 1) for c in (-1, 0, 1)]
BACKWARD = [o for o in ALL if o not in FORWARD]


def iota(shape, dim):
    return lax.broadcasted_iota(jnp.int32, shape, dim)


def xsh(f, by):
    if by == 0:
        return f
    return pltpu.roll(f, 7 if by == 1 else 1, f.ndim - 2)


def zsh(f, by, d):
    if by == 0:
        return f
    lane = iota(f.shape, f.ndim - 1)
    if by == 1:
        return jnp.where(lane < 128 - d, pltpu.roll(f, 128 - d, f.ndim - 1), 0.0)
    return jnp.where(lane >= d, pltpu.roll(f, d, f.ndim - 1), 0.0)


def face(a, b):
    return 1.0 + jnp.square(0.5 * (a + b))


def kernel_body(n, m, x_ref, f_ref, o_ref, s):
    gx, gy = lax.axis_index("gx"), lax.axis_index("gy")

    def device(a, b):
        return (lax.rem(gx + a + n, n), lax.rem(gy + b + m, m))

    started = []

    def send(src, dst, number, a, b):
        copy = pltpu.make_async_remote_copy(
            src_ref=src,
            dst_ref=dst,
            send_sem=s.ssem.at[number],
            recv_sem=s.rsem.at[number],
            device_id=device(a, b),
            device_id_type=MESH,
        )
        copy.start()
        started.append(copy)
        return copy

    def inside(first, shape, width):
        rows = gy * width + first + iota(shape, 0)
        return (rows >= 0) & (rows < m * width)

    barrier = pltpu.get_barrier_semaphore()
    for a, b in GREETED:
        pl.semaphore_signal(barrier, inc=1, device_id=device(a, b), device_id_type=MESH)

    here_x = {-1: pl.ds(0, 4), 0: pl.ds(0, 8), 1: pl.ds(4, 4)}
    there_x = {-1: pl.ds(12, 4), 0: pl.ds(4, 8), 1: pl.ds(0, 4)}
    here_y = {-1: pl.ds(0, 4), 0: pl.ds(0, 16), 1: pl.ds(12, 4)}
    there_y = {-1: pl.ds(24, 4), 0: pl.ds(8, 16), 1: pl.ds(4, 4)}
    here_fx = {-1: pl.ds(0, 1), 0: pl.ds(0, 8), 1: pl.ds(6, 2)}
    there_fx = {-1: pl.ds(12, 1), 0: pl.ds(4, 8), 1: pl.ds(2, 2)}
    own = [
        pltpu.make_async_copy(ref, raw.at[4:12, 8:24], s.lsem.at[k])
        for k, (ref, raw) in enumerate(((x_ref, s.raw_u), (f_ref, s.raw_f)))
    ]
    for copy in own:
        copy.start()
    pl.semaphore_wait(barrier, len(GREETED))
    round1 = []
    number = 0
    for a, b in ROUND1:
        for ref, raw, hx, tx in (
            (x_ref, s.raw_u, here_x, there_x),
            (f_ref, s.raw_f, here_fx, there_fx),
        ):
            round1.append(
                send(ref.at[hx[a], here_y[b]], raw.at[tx[a], there_y[b]], number, a, b)
            )
            number += 1

    def split(raw, out, plane, tiles):
        for first, rows in tiles:
            lane = iota((rows, 128), 1)
            low = lane < 64
            take_a = jnp.where(low, 2 * lane, 2 * lane - 127)
            take_b = jnp.where(low, 2 * lane + 1, 2 * lane - 128)
            va = raw[plane, first : first + rows, 0:128]
            vb = raw[plane, first : first + rows, 128:256]
            va = jnp.take_along_axis(va, take_a, axis=1, mode="promise_in_bounds")
            vb = jnp.take_along_axis(vb, take_b, axis=1, mode="promise_in_bounds")
            place = ((plane % 2) * 8 + plane // 2) * 32 + first
            out[0, place : place + rows, :] = jnp.where(low, va, vb)
            out[1, place : place + rows, :] = pltpu.roll(jnp.where(low, vb, va), 64, 1)

    for copy in own:
        copy.wait()
    for x in range(4, 12):
        split(s.raw_u, s.split_u, x, ((8, 16),))
        split(s.raw_f, s.split_f, x, ((8, 16),))
    for copy in round1:
        copy.wait_recv()
    for x in range(16):
        tiles = ((0, 8), (24, 8)) if 4 <= x < 12 else ((0, 32),)
        split(s.raw_u, s.split_u, x, tiles)
        if 2 <= x < 13:
            split(s.raw_f, s.split_f, x, tiles)
    for i in range(24):
        keep = inside(i - 4, (1, 8, 128), 16)[0]
        for p in range(4):
            at = pl.ds((p % 2) * 256 + i + 4, 8, stride=32)
            u = s.split_u[p // 2, at, :]
            s.u[p, i] = u if 4 <= i < 20 else jnp.where(keep, u, 0.0)
            s.f[p, i] = s.split_f[p // 2, at, :]
    s.u[:, 24:26] = jnp.zeros((4, 2, 8, 128), F32)

    def faces(i, carry):
        at, above = pl.ds(2 * i, 2), pl.ds(2 * i + 1, 2)
        u = [s.u[p, at] for p in range(4)]
        un = [s.u[p, above] for p in range(4)]
        keep = inside(2 * i - 4, (2, 8, 128), 16)
        first = iota((2, 8, 128), 2) == 0
        sx, sz, szd, ky = [], [], [], []
        for z in range(2):
            ka, kb = face(u[2 * z], u[2 * z + 1]), face(u[2 * z + 1], xsh(u[2 * z], 1))
            s.kx[z, at], s.kx[2 + z, at] = ka, kb
            sx.append(0.25 * (ka + kb))
        for x in range(2):
            ka, kb = face(u[x], u[2 + x]), face(u[2 + x], zsh(u[x], 1, 1))
            s.kz[x, at], s.kz[2 + x, at] = ka, kb
            sz.append(0.25 * (ka + kb))
            szd.append(jnp.where(first, face(u[x], 0.0), zsh(sz[x], -1, 1)))
        for p in range(4):
            ky.append(face(u[p], un[p]))
            s.ky[p, at] = ky[p]

        def mx(f0, f1):
            return f0 + 0.25 * (f1 + xsh(f1, -1)), 0.25 * f1

        def mz(f0, f1):
            return f0 + 0.25 * (f1 + zsh(f1, -1, 1)), 0.25 * f1

        sx0, sxp = mz(sx[0], sx[1])
        t0, tp = mx(sz[0], sz[1])
        d0, dp = mx(szd[0], szd[1])
        for k, value in enumerate((sx0, sxp, t0, tp, t0 + d0, tp + dp)):
            s.g[k, at] = jnp.where(keep, value, 0.0)
        h0, hp = mx(ky[0], ky[1])
        j0, jp = mx(ky[2], ky[3])
        h00, h0p = mz(h0, j0)
        hp0, hpp = mz(hp, jp)
        for k, value in enumerate((h00, h0p, hp0, hpp)):
            s.h[k, at] = value
        return carry

    lax.fori_loop(0, 12, faces, 0, unroll=True)

    def beside(ref, row, k):
        at = pl.ds(row, k)
        v = [ref[p, at] for p in range(4)]
        out = []
        for z in range(2):
            for x in range(2):
                p = 2 * z + x
                ka, kb = s.kx[z, at], s.kx[2 + z, at]
                w = v[2 * z + 1 - x]
                if x == 0:
                    total = ka * w + xsh(kb * w, -1)
                else:
                    total = ka * w + kb * xsh(w, 1)
                ka, kb = s.kz[x, at], s.kz[2 + x, at]
                w = v[2 * (1 - z) + x]
                if z == 0:
                    total += ka * w + zsh(kb * w, -1, 1)
                else:
                    total += ka * w + kb * zsh(w, 1, 1)
                total += s.ky[p, at] * ref[p, pl.ds(row + 1, k)]
                total += s.ky[p, pl.ds(row - 1, k)] * ref[p, pl.ds(row - 1, k)]
                out.append(total)
        return v, out

    def smooth0(i, carry):
        row = 2 + 2 * i
        at = pl.ds(row, 2)
        keep = inside(row - 4, (2, 8, 128), 16)
        first = iota((2, 8, 128), 2) == 0
        v, total = beside(s.u, row, 2)
        for z in range(2):
            for x in range(2):
                p = 2 * z + x
                ka, kb = s.kx[z, at], s.kx[2 + z, at]
                diag = ka + (xsh(kb, -1) if x == 0 else kb)
                ka, kb = s.kz[x, at], s.kz[2 + x, at]
                if z == 0:
                    diag += ka + jnp.where(first, face(v[p], 0.0), zsh(kb, -1, 1))
                else:
                    diag += ka + kb
                diag += s.ky[p, at] + s.ky[p, pl.ds(row - 1, 2)]
                newton = s.f[p, at] - (diag * v[p] - total[p])
                weight = WEIGHT / diag
                s.f[p, at] = newton
                s.d0[p, at] = diag
                s.w0[p, at] = weight
                s.e0[p, at] = jnp.where(keep, weight * newton, 0.0)
        return carry

    lax.fori_loop(0, 10, smooth0, 0, unroll=True)

    def residual0(i, carry):
        row = 3 + 2 * i
        at = pl.ds(row, 2)
        keep = inside(row - 4, (2, 8, 128), 16)
        v, total = beside(s.e0, row, 2)
        r = [s.f[p, at] - (s.d0[p, at] * v[p] - total[p]) for p in range(4)]
        r = [r[x] + 0.5 * (r[2 + x] + zsh(r[2 + x], -1, 1)) for x in range(2)]
        s.r0[at] = jnp.where(keep, r[0] + 0.5 * (r[1] + xsh(r[1], -1)), 0.0)
        return carry

    lax.fori_loop(0, 9, residual0, 0, unroll=True)

    def level1(i, only_up):
        base = 2 * i
        edge = (gy == 0) & (i == 2)
        keep = inside(i - 2, (1, 8, 128), 8)[0]

        def v_of(q, row):
            return 0.25 * (s.h[q, row] + s.h[q, row + 1])

        v = [v_of(q, base) for q in range(4)]
        up = [0.25 * s.g[k, base + 1] for k in range(6)]
        sx0, sxp, t0, tp, p0, pp = up
        arrays = {
            (0, 0): sx0 + xsh(sx0, -1) + p0 - v[0],
            (0, 1): sxp + xsh(sxp, -1) - t0 - v[1],
            (1, 0): pp - sx0 - v[2],
            (1, 1): -sxp - tp - v[3],
        }
        fill(9, i, arrays, keep)
        if only_up:
            return
        vd = [jnp.where(edge, s.h[q, base - 1], v_of(q, base - 2)) for q in range(4)]
        both = [v[q] + vd[q] for q in range(4)]
        sx0, sxp, t0, tp, p0, pp = [
            s.g[k, base] + up[k] + 0.25 * s.g[k, base - 1] for k in range(6)
        ]
        arrays = {
            (0, 0): sx0 + xsh(sx0, -1) + p0 + both[0],
            (0, 1): sxp + xsh(sxp, -1) - t0 + both[1],
            (1, 0): pp - sx0 + both[2],
            (1, 1): both[3] - sxp - tp,
        }
        fill(0, i, arrays, keep)
        s.w1[i] = jnp.where(keep, WEIGHT / arrays[(0, 0)], 0.0)

    def fill(first, i, arrays, keep):
        for key in arrays:
            arrays[key] = jnp.where(keep, arrays[key], 0.0)
        for a in (-1, 0, 1):
            for c in (-1, 0, 1):
                value = zsh(arrays[(abs(a), abs(c))], min(c, 0), 1)
                s.a1[first + 3 * (a + 1) + c + 1, i] = xsh(value, min(a, 0))

    def coefficient1(o, row, k):
        a, b, c = o
        at = 3 * (a + 1) + c + 1
        if b == 0:
            return s.a1[at, pl.ds(row, k)]
        return s.a1[9 + at, pl.ds(row if b == 1 else row - 1, k)]

    level1(0, True)

    def level1_step(i, carry):
        level1(i, False)
        return carry

    lax.fori_loop(1, 11, level1_step, 0, unroll=True)

    sub = iota((8, 128), 0)

    def start1(y, carry):
        row = 4 + 2 * y
        b1 = s.r0[row] + 0.5 * (s.r0[row - 1] + s.r0[row + 1])
        e1 = s.w1[y + 2] * b1
        s.re1[1, y + 2] = jnp.where(sub < 4, pltpu.roll(e1, 6, 0), pltpu.roll(b1, 2, 0))
        return carry

    lax.fori_loop(0, 8, start1, 0, unroll=True)

    mine = {-1: pl.ds(2, 2), 0: pl.ds(2, 8), 1: pl.ds(8, 2)}
    theirs = {-1: pl.ds(10, 2), 0: pl.ds(2, 8), 1: pl.ds(0, 2)}
    round2 = []
    for a, b in AROUND:
        round2.append(send(s.re1.at[1, mine[b]], s.re1.at[1 - a, theirs[b]], number, a, b))
        number += 1

    def coarsen(coefficient, row, d, store):
        def get(o, r):
            return coefficient(o, r, 1)[0]

        y0, y1 = {}, {}
        for a in (-1, 0, 1):
            for c in (-1, 0, 1):
                zero_up = 0.25 * get((a, 0, c), row + 1)
                plus = get((a, 1, c), row)
                y0[a, c] = (
                    get((a, 0, c), row)
                    + zero_up
                    + 0.25 * get((a, 0, c), row - 1)
                    + 0.5
                    * (
                        get((a, -1, c), row)
                        + get((a, -1, c), row + 1)
                        + plus
                        + get((a, 1, c), row - 1)
                    )
                )
                y1[a, c] = 0.5 * (plus + get((a, 1, c), row + 1)) + zero_up

        def three(lo, mid, hi, shift, want):
            out = {}
            q = 0.25 * mid
            lo, hi = 0.5 * lo, 0.5 * hi
            if 0 in want:
                out[0] = mid + lo + hi + shift(q + lo, 1) + shift(q + hi, -1)
            if 1 in want:
                out[1] = hi + shift(q + hi, 1)
            if -1 in want:
                out[-1] = lo + shift(q + lo, -1)
            return out

        def by_z(f, by):
            return zsh(f, by, d)

        for b, table in ((0, y0), (1, y1)):
            xs = {}
            for c in (-1, 0, 1):
                want = (0, 1) if b == 0 else (-1, 0, 1)
                got = three(table[-1, c], table[0, c], table[1, c], xsh, want)
                for a in got:
                    xs[a, c] = got[a]
            for a in (0, 1) if b == 0 else (-1, 0, 1):
                want = (0, 1) if (a, b) == (0, 0) else (-1, 0, 1)
                got = three(xs[a, -1], xs[a, 0], xs[a, 1], by_z, want)
                for c in got:
                    store(FORWARD.index((a, b, c)), got[c])

    def coarsen1(y, carry):
        def store(k, value):
            s.ra2[1, y + 2, k // 4, 2 * (k % 4) : 2 * (k % 4) + 1, :] = value[2:3]
            s.ra2[1, y + 2, k // 4, 2 * (k % 4) + 1 : 2 * (k % 4) + 2, :] = value[4:5]
            if k == 0:
                s.w2own[y] = WEIGHT / value

        coarsen(coefficient1, 2 * y + 2, 1, store)
        return carry

    lax.fori_loop(0, 4, coarsen1, 0, unroll=True)
    mine = {-1: pl.ds(2, 2), 0: pl.ds(2, 4), 1: pl.ds(4, 2)}
    theirs = {-1: pl.ds(6, 2), 0: pl.ds(2, 4), 1: pl.ds(0, 2)}
    round2a = []
    for a, b in AROUND:
        round2a.append(send(s.ra2.at[1, mine[b]], s.ra2.at[1 - a, theirs[b]], number, a, b))
        number += 1
    for b in (-1, 0, 1):
        round2a.append(send(s.ra2.at[1, mine[b], 1], s.ra2.at[3, theirs[b], 1], number, -2, b))
        number += 1

    for copy in round2:
        copy.wait_recv()

    def unpack1(i, carry):
        at = pl.ds(2 * i, 2)
        keep = inside(2 * i - 2, (2, 8, 128), 8)
        sub = iota((2, 8, 128), 1)
        lo, mid, hi = s.re1[0, at], s.re1[1, at], s.re1[2, at]
        e = jnp.where(
            sub < 2,
            pltpu.roll(lo, 6, 1),
            jnp.where(sub < 6, pltpu.roll(mid, 2, 1), pltpu.roll(hi, 6, 1)),
        )
        b = jnp.where(
            sub < 2,
            pltpu.roll(lo, 2, 1),
            jnp.where(sub < 6, pltpu.roll(mid, 6, 1), pltpu.roll(hi, 2, 1)),
        )
        s.e1[at] = jnp.where(keep, e, 0.0)
        s.b1[at] = jnp.where(keep, b, 0.0)
        return carry

    lax.fori_loop(0, 6, unpack1, 0, unroll=True)

    def apply(coefficient, ref, row, k, d):
        total = None
        for b in (-1, 0, 1):
            e = ref[pl.ds(row + b, k)]
            for c in (-1, 0, 1):
                ez = zsh(e, c, d)
                for a in (-1, 0, 1):
                    term = coefficient((a, b, c), row, k) * xsh(ez, a)
                    total = term if total is None else total + term
        return total

    def gather_zx(r, d):
        r = r + 0.5 * (zsh(r, -1, d) + zsh(r, 1, d))
        return r + 0.5 * (xsh(r, -1) + xsh(r, 1))

    def residual1(i, carry):
        row = 1 + i
        keep = inside(row - 2, (1, 8, 128), 8)
        r = s.b1[pl.ds(row, 1)] - apply(coefficient1, s.e1, row, 1, 1)
        s.r1[pl.ds(row, 1)] = jnp.where(keep, gather_zx(r, 1), 0.0)
        return carry

    lax.fori_loop(0, 9, residual1, 0, unroll=True)

    def start2(y, carry):
        row = 2 * y + 2
        b2 = s.r1[row] + 0.5 * (s.r1[row - 1] + s.r1[row + 1])
        e2 = s.w2own[y] * b2
        s.re2[1, y + 2, 0:1, :] = e2[2:3]
        s.re2[1, y + 2, 1:2, :] = e2[4:5]
        s.re2[1, y + 2, 2:3, :] = b2[2:3]
        s.re2[1, y + 2, 3:4, :] = b2[4:5]
        return carry

    lax.fori_loop(0, 4, start2, 0, unroll=True)

    mine = {-1: pl.ds(2, 3), 0: pl.ds(2, 4), 1: pl.ds(4, 2)}
    theirs = {-1: pl.ds(6, 3), 0: pl.ds(2, 4), 1: pl.ds(0, 2)}
    round3 = []
    for a, b in AROUND + [(-2, -1), (-2, 0), (-2, 1)]:
        round3.append(send(s.re2.at[1, mine[b]], s.re2.at[1 - a, theirs[b]], number, a, b))
        number += 1

    for copy in round2a:
        copy.wait_recv()

    def unpack_a2(i, carry):
        at = pl.ds(2 * i, 2)
        keep = inside(2 * i - 2, (2, 8, 128), 4)
        sub = iota((2, 8, 128), 1)
        for t in range(4):
            lo, mid, hi = s.ra2[0, at, t], s.ra2[1, at, t], s.ra2[2, at, t]
            for j in range(4):
                k = 4 * t + j
                if k >= 14:
                    continue

                def rolled(v, to):
                    by = (to - 2 * j) % 8
                    return pltpu.roll(v, by, 1) if by else v

                value = jnp.where(sub < 4, rolled(mid, 2), rolled(hi, 4))
                if t == 1:
                    value = jnp.where(sub < 6, value, rolled(s.ra2[3, at, 1], 6))
                value = jnp.where(sub < 2, rolled(lo, 0), value)
                value = jnp.where(keep, value, 0.0)
                s.a2[k, at] = value
                if k == 0:
                    s.w2[at] = jnp.where(keep, WEIGHT / value, 0.0)
        return carry

    lax.fori_loop(0, 4, unpack_a2, 0, unroll=True)

    def expand(ref, back, row, d):
        for k, (a, b, c) in enumerate(BACKWARD):
            value = ref[FORWARD.index((-a, -b, -c)), pl.ds(row + b, 1)]
            back[k, pl.ds(row, 1)] = xsh(zsh(value, c, d), a)

    def reader(ref, back):
        def coefficient(o, row, k):
            if o in FORWARD:
                return ref[FORWARD.index(o), pl.ds(row, k)]
            return back[BACKWARD.index(o), pl.ds(row, k)]

        return coefficient

    def expand2(i, carry):
        expand(s.a2, s.a2b, i, 2)
        return carry

    lax.fori_loop(1, 8, expand2, 0, unroll=True)
    coefficient2 = reader(s.a2, s.a2b)

    def coarsen2(y, carry):
        def store(k, value):
            s.a3own[k, y] = value

        coarsen(coefficient2, 2 * y + 2, 2, store)
        return carry

    lax.fori_loop(0, 2, coarsen2, 0, unroll=True)
    lane = iota((8, 128), 1)
    middle = pl.ds(24, 8)
    for y in range(2):
        for q in range(4):
            value = s.a3own[4 * q, y]
            for j in range(1, 4):
                if 4 * q + j < 14:
                    other = pltpu.roll(s.a3own[4 * q + j, y], j, 1)
                    value = jnp.where(lane % 4 == j, other, value)
            s.ra3[2, 24 + 4 * y + q : 25 + 4 * y + q, :] = value[2:3]

    def send_wide(ref, number):
        copies = []
        for a, b in WIDE:
            copies.append(send(ref.at[2, middle], ref.at[2 + b, pl.ds(8 * (a + 3), 8)], number, -a, -b))
            number += 1
        return copies, number

    round3a, number = send_wide(s.ra3, number)

    for copy in round3:
        copy.wait_recv()
    for k in range(4):
        at = slice(2 * k, 2 * k + 2)
        keep = inside(-2, (9, 2, 128), 4)
        s.e2[0:9, at, :] = jnp.where(keep, s.re2[k, 0:9, 0:2, :], 0.0)
        s.b2[0:9, at, :] = jnp.where(keep, s.re2[k, 0:9, 2:4, :], 0.0)

    def residual2(i, carry):
        row = 1 + i
        keep = inside(row - 2, (1, 8, 128), 4)
        r = s.b2[pl.ds(row, 1)] - apply(coefficient2, s.e2, row, 1, 2)
        s.r2[pl.ds(row, 1)] = jnp.where(keep, gather_zx(r, 2), 0.0)
        return carry

    lax.fori_loop(0, 5, residual2, 0, unroll=True)
    for y in range(2):
        row = 2 * y + 2
        b3 = s.r2[row] + 0.5 * (s.r2[row - 1] + s.r2[row + 1])
        e3 = WEIGHT * b3 / s.a3own[0, y]
        s.rb3[2, 24 + y : 25 + y, :] = b3[2:3]
        s.rb3[2, 26 + y : 27 + y, :] = e3[2:3]

    round4, number = send_wide(s.rb3, number)
    for copy in round3a:
        copy.wait_recv()

    for dy in range(5):
        for y in range(2):
            row = 2 * dy + y
            keep = inside(row - 4, (1, 8, 128), 2)[0]
            for q in range(4):
                value = jnp.where(keep, s.ra3[dy, pl.ds(4 * y + q, 8, stride=8), :], 0.0)
                for j in range(4):
                    if 4 * q + j < 14:
                        s.a3[4 * q + j, row] = pltpu.roll(value, 128 - j, 1) if j else value
            s.w3[row] = jnp.where(keep, WEIGHT / s.a3[0, row], 0.0)

    def expand3(i, carry):
        expand(s.a3, s.a3b, i, 4)
        return carry

    lax.fori_loop(2, 9, expand3, 0, unroll=True)
    coefficient3 = reader(s.a3, s.a3b)

    for copy in round4:
        copy.wait_recv()
    for dy in range(5):
        for y in range(2):
            row = 2 * dy + y
            keep = inside(row - 4, (1, 8, 128), 2)[0]
            b3 = s.rb3[dy, pl.ds(y, 8, stride=8), :]
            e3 = s.rb3[dy, pl.ds(2 + y, 8, stride=8), :]
            s.b3[row] = jnp.where(keep, b3, 0.0)
            s.e3[0, row] = jnp.where(keep, e3, 0.0)

    def sweep(source, target, low, high):
        def step(row, carry):
            at = pl.ds(row, 1)
            old, new = s.e3.at[source], s.e3.at[target]
            r = s.b3[at] - apply(coefficient3, old, row, 1, 4)
            new[at] = old[at] + s.w3[at] * r
            return carry

        lax.fori_loop(low + 4, high + 5, step, 0, unroll=True)

    sweep(0, 1, -2, 3)
    sweep(1, 0, -1, 2)
    sweep(0, 1, 0, 1)
    for y in range(2):
        s.re3[2, 24 + y : 25 + y, :] = s.e3[1, 4 + y, 3:4, :]

    round5, number = send_wide(s.re3, number)
    for copy in round5:
        copy.wait_recv()
    for dy in range(5):
        for y in range(2):
            row = 2 * dy + y
            keep = inside(row - 4, (1, 8, 128), 2)[0]
            e3 = s.re3[dy, pl.ds(y, 8, stride=8), :]
            s.e3[0, row] = jnp.where(keep, e3, 0.0)
    sweep(0, 1, -2, 4)
    sweep(1, 0, -1, 3)

    def spread(c, first, d, place):
        rows = c.shape[0]
        half = 0.5 * (c + xsh(c, 1))
        for k in range(4):
            place[0:rows, 2 * k : 2 * k + 1, :] = c[:, first + k : first + k + 1]
            place[0:rows, 2 * k + 1 : 2 * k + 2, :] = half[:, first + k : first + k + 1]
        value = place[0:rows]
        coarse = iota(value.shape, 2) % (2 * d) == 0
        place[0:rows] = jnp.where(coarse, value, 0.5 * (zsh(value, -1, d) + zsh(value, 1, d)))

    def add_rows(place, rows, target, width):
        for i in range(rows):
            value = place[i // 2]
            if i % 2:
                value = 0.5 * (value + place[i // 2 + 1])
            keep = inside(i - 2, (1, 8, 128), width)[0]
            target[i] = target[i] + jnp.where(keep, value, 0.0)

    spread(s.e3[0, 3:8], 2, 2, s.place)
    add_rows(s.place, 9, s.e2, 4)

    def post2(row, carry):
        at = pl.ds(row, 1)
        r = s.b2[at] - apply(coefficient2, s.e2, row, 1, 2)
        s.x2[at] = s.e2[at] + s.w2[at] * r
        return carry

    lax.fori_loop(1, 8, post2, 0, unroll=True)
    spread(s.x2[1:8], 1, 1, s.place)
    add_rows(s.place, 12, s.e1, 8)

    def post1(i, carry):
        row = 1 + i
        at = pl.ds(row, 1)
        r = s.b1[at] - apply(coefficient1, s.e1, row, 1, 1)
        s.x1[at] = s.e1[at] + s.w1[at] * r
        return carry

    lax.fori_loop(0, 10, post1, 0, unroll=True)
    s.x1[11] = jnp.zeros((8, 128), F32)

    def prolong0(i, carry):
        c = s.x1[i]
        for step in range(2):
            row = 2 * i + step
            keep = inside(row - 4, (1, 8, 128), 16)[0]
            if step:
                c = 0.5 * (c + s.x1[i + 1])
            cz = 0.5 * (c + zsh(c, 1, 1))
            values = (c, 0.5 * (c + xsh(c, 1)), cz, 0.5 * (cz + xsh(cz, 1)))
            for p in range(4):
                s.e0[p, row] = s.e0[p, row] + jnp.where(keep, values[p], 0.0)
        return carry

    lax.fori_loop(1, 11, prolong0, 0, unroll=True)

    def finish(i, carry):
        row = 4 + 2 * i
        at = pl.ds(row, 2)
        v, total = beside(s.e0, row, 2)
        sub = iota((2, 8, 128), 1)
        for z in range(2):
            done = []
            for x in range(2):
                p = 2 * z + x
                r = s.f[p, at] - (s.d0[p, at] * v[p] - total[p])
                value = s.u[p, at] + (v[p] + s.w0[p, at] * r)
                done.append(pltpu.roll(value, 6 if x == 0 else 2, 1))
            both = jnp.where(sub < 4, done[0], done[1])
            for k in range(2):
                s.co[z, pl.ds(pl.multiple_of(16 * i + 8 * k, 8), 8), :] = both[k]
        return carry

    lax.fori_loop(0, 8, finish, 0, unroll=True)

    lane = iota((16, 128), 1)
    low = lane < 64
    take = jnp.where(lane % 2 == 0, lane // 2, 64 + lane // 2)
    for x in range(8):
        place = (x % 2) * 4 + x // 2
        even = s.co[0, pl.ds(place, 16, stride=8), :]
        odd = pltpu.roll(s.co[1, pl.ds(place, 16, stride=8), :], 64, 1)
        va, vb = jnp.where(low, even, odd), pltpu.roll(jnp.where(low, odd, even), 64, 1)
        o_ref[x, :, 0:128] = jnp.take_along_axis(va, take, axis=1, mode="promise_in_bounds")
        o_ref[x, :, 128:256] = jnp.take_along_axis(vb, take, axis=1, mode="promise_in_bounds")
    for copy in started:
        copy.wait_send()


COPIES = 16 + 8 + 11 + 11 + 3 * len(WIDE)
TILE = (8, 128)
SHAPES = {
    "raw_u": (16, 32, 256),
    "raw_f": (16, 32, 256),
    "split_u": (2, 512, 128),
    "split_f": (2, 512, 128),
    "co": (2, 128, 128),
    "u": (4, 26) + TILE,
    "f": (4, 26) + TILE,
    "kx": (4, 24) + TILE,
    "kz": (4, 24) + TILE,
    "ky": (4, 24) + TILE,
    "g": (6, 24) + TILE,
    "h": (4, 24) + TILE,
    "d0": (4, 24) + TILE,
    "w0": (4, 24) + TILE,
    "e0": (4, 26) + TILE,
    "r0": (24,) + TILE,
    "a1": (18, 12) + TILE,
    "w1": (12,) + TILE,
    "re1": (3, 12) + TILE,
    "e1": (12,) + TILE,
    "b1": (12,) + TILE,
    "x1": (12,) + TILE,
    "r1": (12,) + TILE,
    "ra2": (4, 8, 4) + TILE,
    "w2own": (4,) + TILE,
    "a2": (14, 8) + TILE,
    "a2b": (13, 8) + TILE,
    "w2": (8,) + TILE,
    "re2": (4, 9) + TILE,
    "e2": (9,) + TILE,
    "b2": (9,) + TILE,
    "x2": (9,) + TILE,
    "r2": (9,) + TILE,
    "a3own": (14, 2) + TILE,
    "ra3": (5, 64, 128),
    "rb3": (5, 64, 128),
    "re3": (5, 64, 128),
    "a3": (14, 10) + TILE,
    "a3b": (13, 10) + TILE,
    "w3": (10,) + TILE,
    "b3": (10,) + TILE,
    "e3": (2, 10) + TILE,
    "place": (8,) + TILE,
}


class Scratch:
    pass


def on_device(n, m, state, forcing):
    names = list(SHAPES)

    def body(x_ref, f_ref, o_ref, *scratch):
        s = Scratch()
        for name, ref in zip(names, scratch):
            setattr(s, name, ref)
        s.ssem, s.rsem, s.lsem = scratch[len(names) :]
        kernel_body(n, m, x_ref, f_ref, o_ref, s)

    return pl.pallas_call(
        body,
        out_shape=jax.ShapeDtypeStruct(state.shape, F32),
        in_specs=[pl.BlockSpec(memory_space=pl.ANY)] * 2,
        out_specs=pl.BlockSpec(memory_space=pltpu.VMEM),
        scratch_shapes=[pltpu.VMEM(shape, F32) for shape in SHAPES.values()]
        + [pltpu.SemaphoreType.DMA((COPIES,))] * 2
        + [pltpu.SemaphoreType.DMA((2,))],
        compiler_params=pltpu.CompilerParams(
            collective_id=0, has_side_effects=True, vmem_limit_bytes=48 << 20
        ),
    )(*[pltpu.with_memory_space_constraint(v, pltpu.HBM) for v in (state, forcing)])


def solution(mesh):
    n, m = mesh.shape["gx"], mesh.shape["gy"]
    return jax.shard_map(
        lambda state, forcing: on_device(n, m, state, forcing),
        mesh=mesh,
        in_specs=(P("gx", "gy", None), P("gx", "gy", None)),
        out_specs=P("gx", "gy", None),
        check_vma=False,
    )
```

```python
import jax
import jax.numpy as jnp
from jax import lax
from jax.experimental import pallas as pl
from jax.experimental.pallas import tpu as pltpu
from jax.sharding import PartitionSpec as P

WEIGHT = 0.6
MESH = pl.DeviceIdType.MESH
F32 = jnp.float32

AROUND = [(-1, -1), (-1, 1), (1, -1), (1, 1), (0, -1), (0, 1), (-1, 0), (1, 0)]
GREETED = AROUND + [(2, 0)]
WIDE = sorted(
    [(a, b) for a in range(-3, 5) for b in range(-2, 3) if (a, b) != (0, 0)],
    key=lambda o: -(abs(o[0]) + 2 * abs(o[1])),
)
FORWARD = [(0, 0, 0), (0, 0, 1), (1, 0, -1), (1, 0, 0), (1, 0, 1)] + [
    (a, 1, c) for a in (-1, 0, 1) for c in (-1, 0, 1)
]
ALL = [(a, b, c) for b in (-1, 0, 1) for a in (-1, 0, 1) for c in (-1, 0, 1)]
BACKWARD = [o for o in ALL if o not in FORWARD]


def iota(shape, dim):
    return lax.broadcasted_iota(jnp.int32, shape, dim)


def xsh(f, by):
    if by == 0:
        return f
    return pltpu.roll(f, 7 if by == 1 else 1, f.ndim - 2)


def zsh(f, by, d):
    if by == 0:
        return f
    lane = iota(f.shape, f.ndim - 1)
    if by == 1:
        return jnp.where(lane < 128 - d, pltpu.roll(f, 128 - d, f.ndim - 1), 0.0)
    return jnp.where(lane >= d, pltpu.roll(f, d, f.ndim - 1), 0.0)


def face(a, b):
    return 1.0 + jnp.square(0.5 * (a + b))


def kernel_body(n, m, x_ref, f_ref, o_ref, s):
    gx, gy = lax.axis_index("gx"), lax.axis_index("gy")

    def device(a, b):
        return (lax.rem(gx + a + n, n), lax.rem(gy + b + m, m))

    started = []

    def send(src, dst, number, a, b):
        copy = pltpu.make_async_remote_copy(
            src_ref=src,
            dst_ref=dst,
            send_sem=s.ssem.at[number],
            recv_sem=s.rsem.at[number],
            device_id=device(a, b),
            device_id_type=MESH,
        )
        copy.start()
        started.append(copy)
        return copy

    def inside(first, shape, width):
        rows = gy * width + first + iota(shape, 0)
        return (rows >= 0) & (rows < m * width)

    barrier = pltpu.get_barrier_semaphore()
    for a, b in GREETED:
        pl.semaphore_signal(barrier, inc=1, device_id=device(a, b), device_id_type=MESH)

    here_x = {-1: pl.ds(0, 4), 0: pl.ds(0, 8), 1: pl.ds(4, 4)}
    there_x = {-1: pl.ds(12, 4), 0: pl.ds(4, 8), 1: pl.ds(0, 4)}
    here_y = {-1: pl.ds(0, 4), 0: pl.ds(0, 16), 1: pl.ds(12, 4)}
    there_y = {-1: pl.ds(24, 4), 0: pl.ds(8, 16), 1: pl.ds(4, 4)}
    here_fx = {-1: pl.ds(0, 1), 0: pl.ds(0, 8), 1: pl.ds(6, 2)}
    there_fx = {-1: pl.ds(12, 1), 0: pl.ds(4, 8), 1: pl.ds(2, 2)}
    own = [
        pltpu.make_async_copy(ref, raw.at[4:12, 8:24], s.lsem.at[k])
        for k, (ref, raw) in enumerate(((x_ref, s.raw_u), (f_ref, s.raw_f)))
    ]
    for copy in own:
        copy.start()
    pl.semaphore_wait(barrier, len(GREETED))
    round1 = []
    number = 0
    for a, b in AROUND:
        for ref, raw, hx, tx in (
            (x_ref, s.raw_u, here_x, there_x),
            (f_ref, s.raw_f, here_fx, there_fx),
        ):
            round1.append(
                send(ref.at[hx[a], here_y[b]], raw.at[tx[a], there_y[b]], number, a, b)
            )
            number += 1

    def split(raw, out, plane, tiles):
        for first, rows in tiles:
            lane = iota((rows, 128), 1)
            low = lane < 64
            take_a = jnp.where(low, 2 * lane, 2 * lane - 127)
            take_b = jnp.where(low, 2 * lane + 1, 2 * lane - 128)
            va = raw[plane, first : first + rows, 0:128]
            vb = raw[plane, first : first + rows, 128:256]
            va = jnp.take_along_axis(va, take_a, axis=1, mode="promise_in_bounds")
            vb = jnp.take_along_axis(vb, take_b, axis=1, mode="promise_in_bounds")
            place = ((plane % 2) * 8 + plane // 2) * 32 + first
            out[0, place : place + rows, :] = jnp.where(low, va, vb)
            out[1, place : place + rows, :] = pltpu.roll(jnp.where(low, vb, va), 64, 1)

    for copy in own:
        copy.wait()
    for x in range(4, 12):
        split(s.raw_u, s.split_u, x, ((8, 16),))
        split(s.raw_f, s.split_f, x, ((8, 16),))
    def split_planes(planes, tiles):
        for x in planes:
            split(s.raw_u, s.split_u, x, tiles)
            if 2 <= x < 13:
                split(s.raw_f, s.split_f, x, tiles)

    def collect(rows, outer):
        for i in rows:
            keep = inside(i - 4, (1, 8, 128), 16)[0]
            for p in range(4):
                at = pl.ds((p % 2) * 256 + i + 4, 8, stride=32)
                u = s.split_u[p // 2, at, :]
                s.u[p, i] = jnp.where(keep, u, 0.0) if outer else u
                if 2 <= i < 22:
                    s.f[p, i] = s.split_f[p // 2, at, :]

    outside_x = (0, 1, 2, 3, 12, 13, 14, 15)
    for copy in round1[12:16]:
        copy.wait_recv()
    split_planes(outside_x, ((8, 16),))
    collect(range(4, 20), False)
    for copy in round1[8:12]:
        copy.wait_recv()
    split_planes(range(4, 12), ((0, 8), (24, 8)))
    for copy in round1[0:8]:
        copy.wait_recv()
    split_planes(outside_x, ((0, 8), (24, 8)))
    collect((0, 1, 2, 3, 20, 21, 22, 23), True)
    s.u[:, 24:26] = jnp.zeros((4, 2, 8, 128), F32)

    def faces(i, carry):
        at, above = pl.ds(2 * i, 2), pl.ds(2 * i + 1, 2)
        u = [s.u[p, at] for p in range(4)]
        un = [s.u[p, above] for p in range(4)]
        keep = inside(2 * i - 4, (2, 8, 128), 16)
        first = iota((2, 8, 128), 2) == 0
        sx, sz, szd, ky = [], [], [], []
        for z in range(2):
            ka, kb = face(u[2 * z], u[2 * z + 1]), face(u[2 * z + 1], xsh(u[2 * z], 1))
            s.kx[z, at], s.kx[2 + z, at] = ka, kb
            sx.append(0.25 * (ka + kb))
        for x in range(2):
            ka, kb = face(u[x], u[2 + x]), face(u[2 + x], zsh(u[x], 1, 1))
            s.kz[x, at], s.kz[2 + x, at] = ka, kb
            sz.append(0.25 * (ka + kb))
            szd.append(jnp.where(first, face(u[x], 0.0), zsh(sz[x], -1, 1)))
        for p in range(4):
            ky.append(face(u[p], un[p]))
            s.ky[p, at] = ky[p]

        def mx(f0, f1):
            return f0 + 0.25 * (f1 + xsh(f1, -1)), 0.25 * f1

        def mz(f0, f1):
            return f0 + 0.25 * (f1 + zsh(f1, -1, 1)), 0.25 * f1

        sx0, sxp = mz(sx[0], sx[1])
        t0, tp = mx(sz[0], sz[1])
        d0, dp = mx(szd[0], szd[1])
        for k, value in enumerate((sx0, sxp, t0, tp, t0 + d0, tp + dp)):
            s.g[k, at] = jnp.where(keep, value, 0.0)
        h0, hp = mx(ky[0], ky[1])
        j0, jp = mx(ky[2], ky[3])
        h00, h0p = mz(h0, j0)
        hp0, hpp = mz(hp, jp)
        for k, value in enumerate((h00, h0p, hp0, hpp)):
            s.h[k, at] = value
        return carry

    lax.fori_loop(0, 12, faces, 0, unroll=True)

    def beside(ref, row, k):
        at = pl.ds(row, k)
        v = [ref[p, at] for p in range(4)]
        out = []
        for z in range(2):
            for x in range(2):
                p = 2 * z + x
                ka, kb = s.kx[z, at], s.kx[2 + z, at]
                w = v[2 * z + 1 - x]
                if x == 0:
                    total = ka * w + xsh(kb * w, -1)
                else:
                    total = ka * w + kb * xsh(w, 1)
                ka, kb = s.kz[x, at], s.kz[2 + x, at]
                w = v[2 * (1 - z) + x]
                if z == 0:
                    total += ka * w + zsh(kb * w, -1, 1)
                else:
                    total += ka * w + kb * zsh(w, 1, 1)
                total += s.ky[p, at] * ref[p, pl.ds(row + 1, k)]
                total += s.ky[p, pl.ds(row - 1, k)] * ref[p, pl.ds(row - 1, k)]
                out.append(total)
        return v, out

    def smooth0(i, carry):
        row = 2 + 2 * i
        at = pl.ds(row, 2)
        keep = inside(row - 4, (2, 8, 128), 16)
        first = iota((2, 8, 128), 2) == 0
        v, total = beside(s.u, row, 2)
        for z in range(2):
            for x in range(2):
                p = 2 * z + x
                ka, kb = s.kx[z, at], s.kx[2 + z, at]
                diag = ka + (xsh(kb, -1) if x == 0 else kb)
                ka, kb = s.kz[x, at], s.kz[2 + x, at]
                if z == 0:
                    diag += ka + jnp.where(first, face(v[p], 0.0), zsh(kb, -1, 1))
                else:
                    diag += ka + kb
                diag += s.ky[p, at] + s.ky[p, pl.ds(row - 1, 2)]
                newton = s.f[p, at] - (diag * v[p] - total[p])
                weight = WEIGHT / diag
                s.f[p, at] = newton
                s.d0[p, at] = diag
                s.w0[p, at] = weight
                s.e0[p, at] = jnp.where(keep, weight * newton, 0.0)
        return carry

    lax.fori_loop(0, 10, smooth0, 0, unroll=True)

    def residual0(i, carry):
        row = 3 + 2 * i
        at = pl.ds(row, 2)
        keep = inside(row - 4, (2, 8, 128), 16)
        v, total = beside(s.e0, row, 2)
        r = [s.f[p, at] - (s.d0[p, at] * v[p] - total[p]) for p in range(4)]
        r = [r[x] + 0.5 * (r[2 + x] + zsh(r[2 + x], -1, 1)) for x in range(2)]
        s.r0[at] = jnp.where(keep, r[0] + 0.5 * (r[1] + xsh(r[1], -1)), 0.0)
        return carry

    lax.fori_loop(0, 9, residual0, 0, unroll=True)

    def level1(i, only_up):
        base = 2 * i
        edge = (gy == 0) & (i == 2)
        keep = inside(i - 2, (1, 8, 128), 8)[0]

        def v_of(q, row):
            return 0.25 * (s.h[q, row] + s.h[q, row + 1])

        v = [v_of(q, base) for q in range(4)]
        up = [0.25 * s.g[k, base + 1] for k in range(6)]
        sx0, sxp, t0, tp, p0, pp = up
        arrays = {
            (0, 0): sx0 + xsh(sx0, -1) + p0 - v[0],
            (0, 1): sxp + xsh(sxp, -1) - t0 - v[1],
            (1, 0): pp - sx0 - v[2],
            (1, 1): -sxp - tp - v[3],
        }
        fill(9, i, arrays, keep)
        if only_up:
            return
        vd = [jnp.where(edge, s.h[q, base - 1], v_of(q, base - 2)) for q in range(4)]
        both = [v[q] + vd[q] for q in range(4)]
        sx0, sxp, t0, tp, p0, pp = [
            s.g[k, base] + up[k] + 0.25 * s.g[k, base - 1] for k in range(6)
        ]
        arrays = {
            (0, 0): sx0 + xsh(sx0, -1) + p0 + both[0],
            (0, 1): sxp + xsh(sxp, -1) - t0 + both[1],
            (1, 0): pp - sx0 + both[2],
            (1, 1): both[3] - sxp - tp,
        }
        fill(0, i, arrays, keep)
        s.w1[i] = jnp.where(keep, WEIGHT / arrays[(0, 0)], 0.0)

    def fill(first, i, arrays, keep):
        for key in arrays:
            arrays[key] = jnp.where(keep, arrays[key], 0.0)
        for a in (-1, 0, 1):
            for c in (-1, 0, 1):
                value = zsh(arrays[(abs(a), abs(c))], min(c, 0), 1)
                s.a1[first + 3 * (a + 1) + c + 1, i] = xsh(value, min(a, 0))

    def coefficient1(o, row, k):
        a, b, c = o
        at = 3 * (a + 1) + c + 1
        if b == 0:
            return s.a1[at, pl.ds(row, k)]
        return s.a1[9 + at, pl.ds(row if b == 1 else row - 1, k)]

    level1(0, True)

    def level1_step(i, carry):
        level1(i, False)
        return carry

    lax.fori_loop(1, 11, level1_step, 0, unroll=True)

    sub = iota((8, 128), 0)

    def start1(y, carry):
        row = 4 + 2 * y
        b1 = s.r0[row] + 0.5 * (s.r0[row - 1] + s.r0[row + 1])
        e1 = s.w1[y + 2] * b1
        s.re1[1, y + 2] = jnp.where(sub < 4, pltpu.roll(e1, 6, 0), pltpu.roll(b1, 2, 0))
        return carry

    lax.fori_loop(0, 8, start1, 0, unroll=True)

    mine = {-1: pl.ds(2, 2), 0: pl.ds(2, 8), 1: pl.ds(8, 2)}
    theirs = {-1: pl.ds(10, 2), 0: pl.ds(2, 8), 1: pl.ds(0, 2)}
    round2 = []
    for a, b in AROUND:
        round2.append(send(s.re1.at[1, mine[b]], s.re1.at[1 - a, theirs[b]], number, a, b))
        number += 1

    def coarsen(coefficient, row, d, store):
        def get(o, r):
            return coefficient(o, r, 1)[0]

        y0, y1 = {}, {}
        for a in (-1, 0, 1):
            for c in (-1, 0, 1):
                zero_up = 0.25 * get((a, 0, c), row + 1)
                plus = get((a, 1, c), row)
                y0[a, c] = (
                    get((a, 0, c), row)
                    + zero_up
                    + 0.25 * get((a, 0, c), row - 1)
                    + 0.5
                    * (
                        get((a, -1, c), row)
                        + get((a, -1, c), row + 1)
                        + plus
                        + get((a, 1, c), row - 1)
                    )
                )
                y1[a, c] = 0.5 * (plus + get((a, 1, c), row + 1)) + zero_up

        def three(lo, mid, hi, shift, want):
            out = {}
            q = 0.25 * mid
            lo, hi = 0.5 * lo, 0.5 * hi
            if 0 in want:
                out[0] = mid + lo + hi + shift(q + lo, 1) + shift(q + hi, -1)
            if 1 in want:
                out[1] = hi + shift(q + hi, 1)
            if -1 in want:
                out[-1] = lo + shift(q + lo, -1)
            return out

        def by_z(f, by):
            return zsh(f, by, d)

        for b, table in ((0, y0), (1, y1)):
            xs = {}
            for c in (-1, 0, 1):
                want = (0, 1) if b == 0 else (-1, 0, 1)
                got = three(table[-1, c], table[0, c], table[1, c], xsh, want)
                for a in got:
                    xs[a, c] = got[a]
            for a in (0, 1) if b == 0 else (-1, 0, 1):
                want = (0, 1) if (a, b) == (0, 0) else (-1, 0, 1)
                got = three(xs[a, -1], xs[a, 0], xs[a, 1], by_z, want)
                for c in got:
                    store(FORWARD.index((a, b, c)), got[c])

    def coarsen1(y, carry):
        def store(k, value):
            s.ra2[1, y + 2, k // 4, 2 * (k % 4) : 2 * (k % 4) + 1, :] = value[2:3]
            s.ra2[1, y + 2, k // 4, 2 * (k % 4) + 1 : 2 * (k % 4) + 2, :] = value[4:5]
            if k == 0:
                s.w2own[y] = WEIGHT / value

        coarsen(coefficient1, 2 * y + 2, 1, store)
        return carry

    lax.fori_loop(0, 4, coarsen1, 0, unroll=True)
    mine = {-1: pl.ds(2, 2), 0: pl.ds(2, 4), 1: pl.ds(4, 2)}
    theirs = {-1: pl.ds(6, 2), 0: pl.ds(2, 4), 1: pl.ds(0, 2)}
    round2a = []
    for a, b in AROUND:
        round2a.append(send(s.ra2.at[1, mine[b]], s.ra2.at[1 - a, theirs[b]], number, a, b))
        number += 1
    for b in (-1, 0, 1):
        round2a.append(send(s.ra2.at[1, mine[b], 1], s.ra2.at[3, theirs[b], 1], number, -2, b))
        number += 1

    for copy in round2:
        copy.wait_recv()

    def unpack1(i, carry):
        at = pl.ds(2 * i, 2)
        keep = inside(2 * i - 2, (2, 8, 128), 8)
        sub = iota((2, 8, 128), 1)
        lo, mid, hi = s.re1[0, at], s.re1[1, at], s.re1[2, at]
        e = jnp.where(
            sub < 2,
            pltpu.roll(lo, 6, 1),
            jnp.where(sub < 6, pltpu.roll(mid, 2, 1), pltpu.roll(hi, 6, 1)),
        )
        b = jnp.where(
            sub < 2,
            pltpu.roll(lo, 2, 1),
            jnp.where(sub < 6, pltpu.roll(mid, 6, 1), pltpu.roll(hi, 2, 1)),
        )
        s.e1[at] = jnp.where(keep, e, 0.0)
        s.b1[at] = jnp.where(keep, b, 0.0)
        return carry

    lax.fori_loop(0, 6, unpack1, 0, unroll=True)

    def apply(coefficient, ref, row, k, d):
        total = None
        for b in (-1, 0, 1):
            e = ref[pl.ds(row + b, k)]
            for c in (-1, 0, 1):
                ez = zsh(e, c, d)
                for a in (-1, 0, 1):
                    term = coefficient((a, b, c), row, k) * xsh(ez, a)
                    total = term if total is None else total + term
        return total

    def gather_zx(r, d):
        r = r + 0.5 * (zsh(r, -1, d) + zsh(r, 1, d))
        return r + 0.5 * (xsh(r, -1) + xsh(r, 1))

    def residual1(i, carry):
        row = 1 + i
        keep = inside(row - 2, (1, 8, 128), 8)
        r = s.b1[pl.ds(row, 1)] - apply(coefficient1, s.e1, row, 1, 1)
        s.r1[pl.ds(row, 1)] = jnp.where(keep, gather_zx(r, 1), 0.0)
        return carry

    lax.fori_loop(0, 9, residual1, 0, unroll=True)

    def start2(y, carry):
        row = 2 * y + 2
        b2 = s.r1[row] + 0.5 * (s.r1[row - 1] + s.r1[row + 1])
        e2 = s.w2own[y] * b2
        s.re2[1, y + 2, 0:1, :] = e2[2:3]
        s.re2[1, y + 2, 1:2, :] = e2[4:5]
        s.re2[1, y + 2, 2:3, :] = b2[2:3]
        s.re2[1, y + 2, 3:4, :] = b2[4:5]
        return carry

    lax.fori_loop(0, 4, start2, 0, unroll=True)

    mine = {-1: pl.ds(2, 3), 0: pl.ds(2, 4), 1: pl.ds(4, 2)}
    theirs = {-1: pl.ds(6, 3), 0: pl.ds(2, 4), 1: pl.ds(0, 2)}
    round3 = []
    for a, b in [(-2, -1), (-2, 1)] + AROUND + [(-2, 0)]:
        round3.append(send(s.re2.at[1, mine[b]], s.re2.at[1 - a, theirs[b]], number, a, b))
        number += 1

    for copy in round2a:
        copy.wait_recv()

    def unpack_a2(i, carry):
        at = pl.ds(2 * i, 2)
        keep = inside(2 * i - 2, (2, 8, 128), 4)
        sub = iota((2, 8, 128), 1)
        for t in range(4):
            lo, mid, hi = s.ra2[0, at, t], s.ra2[1, at, t], s.ra2[2, at, t]
            for j in range(4):
                k = 4 * t + j
                if k >= 14:
                    continue

                def rolled(v, to):
                    by = (to - 2 * j) % 8
                    return pltpu.roll(v, by, 1) if by else v

                value = jnp.where(sub < 4, rolled(mid, 2), rolled(hi, 4))
                if t == 1:
                    value = jnp.where(sub < 6, value, rolled(s.ra2[3, at, 1], 6))
                value = jnp.where(sub < 2, rolled(lo, 0), value)
                value = jnp.where(keep, value, 0.0)
                s.a2[k, at] = value
                if k == 0:
                    s.w2[at] = jnp.where(keep, WEIGHT / value, 0.0)
        return carry

    lax.fori_loop(0, 4, unpack_a2, 0, unroll=True)

    def expand(ref, back, row, d):
        for k, (a, b, c) in enumerate(BACKWARD):
            value = ref[FORWARD.index((-a, -b, -c)), pl.ds(row + b, 1)]
            back[k, pl.ds(row, 1)] = xsh(zsh(value, c, d), a)

    def reader(ref, back):
        def coefficient(o, row, k):
            if o in FORWARD:
                return ref[FORWARD.index(o), pl.ds(row, k)]
            return back[BACKWARD.index(o), pl.ds(row, k)]

        return coefficient

    def expand2(i, carry):
        expand(s.a2, s.a2b, i, 2)
        return carry

    lax.fori_loop(1, 8, expand2, 0, unroll=True)
    coefficient2 = reader(s.a2, s.a2b)

    def coarsen2(y, carry):
        def store(k, value):
            s.a3own[k, y] = value

        coarsen(coefficient2, 2 * y + 2, 2, store)
        return carry

    lax.fori_loop(0, 2, coarsen2, 0, unroll=True)
    lane = iota((8, 128), 1)
    middle = pl.ds(24, 8)
    for y in range(2):
        for q in range(4):
            value = s.a3own[4 * q, y]
            for j in range(1, 4):
                if 4 * q + j < 14:
                    other = pltpu.roll(s.a3own[4 * q + j, y], j, 1)
                    value = jnp.where(lane % 4 == j, other, value)
            s.ra3[2, 24 + 4 * y + q : 25 + 4 * y + q, :] = value[2:3]

    def send_wide(ref, number, last=4):
        copies = []
        for a, b in [o for o in WIDE if o[0] <= last]:
            copies.append(send(ref.at[2, middle], ref.at[2 + b, pl.ds(8 * (a + 3), 8)], number, -a, -b))
            number += 1
        return copies, number

    round3a, number = send_wide(s.ra3, number)

    for copy in round3:
        copy.wait_recv()
    for k in range(4):
        at = slice(2 * k, 2 * k + 2)
        keep = inside(-2, (9, 2, 128), 4)
        s.e2[0:9, at, :] = jnp.where(keep, s.re2[k, 0:9, 0:2, :], 0.0)
        s.b2[0:9, at, :] = jnp.where(keep, s.re2[k, 0:9, 2:4, :], 0.0)

    def residual2(i, carry):
        row = 1 + i
        keep = inside(row - 2, (1, 8, 128), 4)
        r = s.b2[pl.ds(row, 1)] - apply(coefficient2, s.e2, row, 1, 2)
        s.r2[pl.ds(row, 1)] = jnp.where(keep, gather_zx(r, 2), 0.0)
        return carry

    lax.fori_loop(0, 5, residual2, 0, unroll=True)
    for y in range(2):
        row = 2 * y + 2
        b3 = s.r2[row] + 0.5 * (s.r2[row - 1] + s.r2[row + 1])
        e3 = WEIGHT * b3 / s.a3own[0, y]
        s.rb3[2, 24 + y : 25 + y, :] = b3[2:3]
        s.rb3[2, 26 + y : 27 + y, :] = e3[2:3]

    round4, number = send_wide(s.rb3, number, 3)
    for copy in round3a:
        copy.wait_recv()

    for dy in range(5):
        for y in range(2):
            row = 2 * dy + y
            keep = inside(row - 4, (1, 8, 128), 2)[0]
            for q in range(4):
                value = jnp.where(keep, s.ra3[dy, pl.ds(4 * y + q, 8, stride=8), :], 0.0)
                for j in range(4):
                    if 4 * q + j < 14:
                        s.a3[4 * q + j, row] = pltpu.roll(value, 128 - j, 1) if j else value
            s.w3[row] = jnp.where(keep, WEIGHT / s.a3[0, row], 0.0)

    def expand3(i, carry):
        expand(s.a3, s.a3b, i, 4)
        return carry

    lax.fori_loop(2, 9, expand3, 0, unroll=True)
    coefficient3 = reader(s.a3, s.a3b)

    for copy in round4:
        copy.wait_recv()
    for dy in range(5):
        for y in range(2):
            row = 2 * dy + y
            keep = inside(row - 4, (1, 8, 128), 2)[0]
            b3 = s.rb3[dy, pl.ds(y, 8, stride=8), :]
            e3 = s.rb3[dy, pl.ds(2 + y, 8, stride=8), :]
            s.b3[row] = jnp.where(keep, b3, 0.0)
            s.e3[0, row] = jnp.where(keep, e3, 0.0)

    def sweep(source, target, low, high):
        def step(row, carry):
            at = pl.ds(row, 1)
            old, new = s.e3.at[source], s.e3.at[target]
            r = s.b3[at] - apply(coefficient3, old, row, 1, 4)
            new[at] = old[at] + s.w3[at] * r
            return carry

        lax.fori_loop(low + 4, high + 5, step, 0, unroll=True)

    sweep(0, 1, -2, 3)
    sweep(1, 0, -1, 2)
    sweep(0, 1, 0, 1)
    for y in range(2):
        s.re3[2, 24 + y : 25 + y, :] = s.e3[1, 4 + y, 3:4, :]

    round5, number = send_wide(s.re3, number)
    for copy in round5:
        copy.wait_recv()
    for dy in range(5):
        for y in range(2):
            row = 2 * dy + y
            keep = inside(row - 4, (1, 8, 128), 2)[0]
            e3 = s.re3[dy, pl.ds(y, 8, stride=8), :]
            s.e3[0, row] = jnp.where(keep, e3, 0.0)
    sweep(0, 1, -2, 4)
    sweep(1, 0, -1, 3)

    def spread(c, first, d, place):
        rows = c.shape[0]
        half = 0.5 * (c + xsh(c, 1))
        for k in range(4):
            place[0:rows, 2 * k : 2 * k + 1, :] = c[:, first + k : first + k + 1]
            place[0:rows, 2 * k + 1 : 2 * k + 2, :] = half[:, first + k : first + k + 1]
        value = place[0:rows]
        coarse = iota(value.shape, 2) % (2 * d) == 0
        place[0:rows] = jnp.where(coarse, value, 0.5 * (zsh(value, -1, d) + zsh(value, 1, d)))

    def add_rows(place, rows, target, width):
        for i in range(rows):
            value = place[i // 2]
            if i % 2:
                value = 0.5 * (value + place[i // 2 + 1])
            keep = inside(i - 2, (1, 8, 128), width)[0]
            target[i] = target[i] + jnp.where(keep, value, 0.0)

    spread(s.e3[0, 3:8], 2, 2, s.place)
    add_rows(s.place, 9, s.e2, 4)

    def post2(row, carry):
        at = pl.ds(row, 1)
        r = s.b2[at] - apply(coefficient2, s.e2, row, 1, 2)
        s.x2[at] = s.e2[at] + s.w2[at] * r
        return carry

    lax.fori_loop(1, 8, post2, 0, unroll=True)
    spread(s.x2[1:8], 1, 1, s.place)
    add_rows(s.place, 12, s.e1, 8)

    def post1(i, carry):
        row = 1 + i
        at = pl.ds(row, 1)
        r = s.b1[at] - apply(coefficient1, s.e1, row, 1, 1)
        s.x1[at] = s.e1[at] + s.w1[at] * r
        return carry

    lax.fori_loop(0, 10, post1, 0, unroll=True)
    s.x1[11] = jnp.zeros((8, 128), F32)

    def prolong0(i, carry):
        c = s.x1[i]
        for step in range(2):
            row = 2 * i + step
            keep = inside(row - 4, (1, 8, 128), 16)[0]
            if step:
                c = 0.5 * (c + s.x1[i + 1])
            cz = 0.5 * (c + zsh(c, 1, 1))
            values = (c, 0.5 * (c + xsh(c, 1)), cz, 0.5 * (cz + xsh(cz, 1)))
            for p in range(4):
                s.e0[p, row] = s.e0[p, row] + jnp.where(keep, values[p], 0.0)
        return carry

    lax.fori_loop(1, 11, prolong0, 0, unroll=True)

    def finish(i, carry):
        row = 4 + 2 * i
        at = pl.ds(row, 2)
        v, total = beside(s.e0, row, 2)
        sub = iota((2, 8, 128), 1)
        for z in range(2):
            done = []
            for x in range(2):
                p = 2 * z + x
                r = s.f[p, at] - (s.d0[p, at] * v[p] - total[p])
                value = s.u[p, at] + (v[p] + s.w0[p, at] * r)
                done.append(pltpu.roll(value, 6 if x == 0 else 2, 1))
            both = jnp.where(sub < 4, done[0], done[1])
            for k in range(2):
                s.co[z, pl.ds(pl.multiple_of(16 * i + 8 * k, 8), 8), :] = both[k]
        return carry

    lax.fori_loop(0, 8, finish, 0, unroll=True)

    lane = iota((16, 128), 1)
    low = lane < 64
    take = jnp.where(lane % 2 == 0, lane // 2, 64 + lane // 2)
    for x in range(8):
        place = (x % 2) * 4 + x // 2
        even = s.co[0, pl.ds(place, 16, stride=8), :]
        odd = pltpu.roll(s.co[1, pl.ds(place, 16, stride=8), :], 64, 1)
        va, vb = jnp.where(low, even, odd), pltpu.roll(jnp.where(low, odd, even), 64, 1)
        o_ref[x, :, 0:128] = jnp.take_along_axis(va, take, axis=1, mode="promise_in_bounds")
        o_ref[x, :, 128:256] = jnp.take_along_axis(vb, take, axis=1, mode="promise_in_bounds")
    for copy in started:
        copy.wait_send()


COPIES = 16 + 8 + 11 + 11 + 3 * len(WIDE)
TILE = (8, 128)
SHAPES = {
    "raw_u": (16, 32, 256),
    "raw_f": (16, 32, 256),
    "split_u": (2, 512, 128),
    "split_f": (2, 512, 128),
    "co": (2, 128, 128),
    "u": (4, 26) + TILE,
    "f": (4, 26) + TILE,
    "kx": (4, 24) + TILE,
    "kz": (4, 24) + TILE,
    "ky": (4, 24) + TILE,
    "g": (6, 24) + TILE,
    "h": (4, 24) + TILE,
    "d0": (4, 24) + TILE,
    "w0": (4, 24) + TILE,
    "e0": (4, 26) + TILE,
    "r0": (24,) + TILE,
    "a1": (18, 12) + TILE,
    "w1": (12,) + TILE,
    "re1": (3, 12) + TILE,
    "e1": (12,) + TILE,
    "b1": (12,) + TILE,
    "x1": (12,) + TILE,
    "r1": (12,) + TILE,
    "ra2": (4, 8, 4) + TILE,
    "w2own": (4,) + TILE,
    "a2": (14, 8) + TILE,
    "a2b": (13, 8) + TILE,
    "w2": (8,) + TILE,
    "re2": (4, 9) + TILE,
    "e2": (9,) + TILE,
    "b2": (9,) + TILE,
    "x2": (9,) + TILE,
    "r2": (9,) + TILE,
    "a3own": (14, 2) + TILE,
    "ra3": (5, 64, 128),
    "rb3": (5, 64, 128),
    "re3": (5, 64, 128),
    "a3": (14, 10) + TILE,
    "a3b": (13, 10) + TILE,
    "w3": (10,) + TILE,
    "b3": (10,) + TILE,
    "e3": (2, 10) + TILE,
    "place": (8,) + TILE,
}


class Scratch:
    pass


def on_device(n, m, state, forcing):
    names = list(SHAPES)

    def body(x_ref, f_ref, o_ref, *scratch):
        s = Scratch()
        for name, ref in zip(names, scratch):
            setattr(s, name, ref)
        s.ssem, s.rsem, s.lsem = scratch[len(names) :]
        kernel_body(n, m, x_ref, f_ref, o_ref, s)

    return pl.pallas_call(
        body,
        out_shape=jax.ShapeDtypeStruct(state.shape, F32),
        in_specs=[pl.BlockSpec(memory_space=pl.ANY)] * 2,
        out_specs=pl.BlockSpec(memory_space=pltpu.VMEM),
        scratch_shapes=[pltpu.VMEM(shape, F32) for shape in SHAPES.values()]
        + [pltpu.SemaphoreType.DMA((COPIES,))] * 2
        + [pltpu.SemaphoreType.DMA((2,))],
        compiler_params=pltpu.CompilerParams(
            collective_id=0, has_side_effects=True, vmem_limit_bytes=48 << 20
        ),
    )(*[pltpu.with_memory_space_constraint(v, pltpu.HBM) for v in (state, forcing)])


def solution(mesh):
    n, m = mesh.shape["gx"], mesh.shape["gy"]
    return jax.shard_map(
        lambda state, forcing: on_device(n, m, state, forcing),
        mesh=mesh,
        in_specs=(P("gx", "gy", None), P("gx", "gy", None)),
        out_specs=P("gx", "gy", None),
        check_vma=False,
    )
```

```python
import jax
import jax.numpy as jnp
from jax import lax
from jax.experimental import pallas as pl
from jax.experimental.pallas import tpu as pltpu
from jax.sharding import PartitionSpec as P

WEIGHT = 0.6
MESH = pl.DeviceIdType.MESH
F32 = jnp.float32

AROUND = [(-1, -1), (-1, 1), (1, -1), (1, 1), (0, -1), (0, 1), (-1, 0), (1, 0)]
GREETED = AROUND + [(2, 0)]
WIDE = sorted(
    [(a, b) for a in range(-3, 5) for b in range(-2, 3) if (a, b) != (0, 0)],
    key=lambda o: -(abs(o[0]) + 2 * abs(o[1])),
)
FORWARD = [(0, 0, 0), (0, 0, 1), (1, 0, -1), (1, 0, 0), (1, 0, 1)] + [
    (a, 1, c) for a in (-1, 0, 1) for c in (-1, 0, 1)
]
ALL = [(a, b, c) for b in (-1, 0, 1) for a in (-1, 0, 1) for c in (-1, 0, 1)]
BACKWARD = [o for o in ALL if o not in FORWARD]


def iota(shape, dim):
    return lax.broadcasted_iota(jnp.int32, shape, dim)


def xsh(f, by):
    if by == 0:
        return f
    return pltpu.roll(f, 7 if by == 1 else 1, f.ndim - 2)


def zsh(f, by, d):
    if by == 0:
        return f
    lane = iota(f.shape, f.ndim - 1)
    if by == 1:
        return jnp.where(lane < 128 - d, pltpu.roll(f, 128 - d, f.ndim - 1), 0.0)
    return jnp.where(lane >= d, pltpu.roll(f, d, f.ndim - 1), 0.0)


def face(a, b):
    return 1.0 + jnp.square(0.5 * (a + b))


def kernel_body(n, m, x_ref, f_ref, o_ref, s):
    gx, gy = lax.axis_index("gx"), lax.axis_index("gy")

    def device(a, b):
        return (lax.rem(gx + a + n, n), lax.rem(gy + b + m, m))

    started = []

    def send(src, dst, number, a, b):
        copy = pltpu.make_async_remote_copy(
            src_ref=src,
            dst_ref=dst,
            send_sem=s.ssem.at[number],
            recv_sem=s.rsem.at[number],
            device_id=device(a, b),
            device_id_type=MESH,
        )
        copy.start()
        started.append(copy)
        return copy

    def inside(first, shape, width):
        rows = gy * width + first + iota(shape, 0)
        return (rows >= 0) & (rows < m * width)

    barrier = pltpu.get_barrier_semaphore()
    for a, b in GREETED:
        pl.semaphore_signal(barrier, inc=1, device_id=device(a, b), device_id_type=MESH)

    here_x = {-1: pl.ds(0, 4), 0: pl.ds(0, 8), 1: pl.ds(4, 4)}
    there_x = {-1: pl.ds(12, 4), 0: pl.ds(4, 8), 1: pl.ds(0, 4)}
    here_y = {-1: pl.ds(0, 4), 0: pl.ds(0, 16), 1: pl.ds(12, 4)}
    there_y = {-1: pl.ds(24, 4), 0: pl.ds(8, 16), 1: pl.ds(4, 4)}
    here_fx = {-1: pl.ds(0, 1), 0: pl.ds(0, 8), 1: pl.ds(6, 2)}
    there_fx = {-1: pl.ds(12, 1), 0: pl.ds(4, 8), 1: pl.ds(2, 2)}
    own = [
        pltpu.make_async_copy(ref, raw.at[4:12, 8:24], s.lsem.at[k])
        for k, (ref, raw) in enumerate(((x_ref, s.raw_u), (f_ref, s.raw_f)))
    ]
    for copy in own:
        copy.start()
    pl.semaphore_wait(barrier, len(GREETED))
    round1 = []
    number = 0
    for a, b in AROUND:
        for ref, raw, hx, tx in (
            (x_ref, s.raw_u, here_x, there_x),
            (f_ref, s.raw_f, here_fx, there_fx),
        ):
            round1.append(
                send(ref.at[hx[a], here_y[b]], raw.at[tx[a], there_y[b]], number, a, b)
            )
            number += 1

    def split(raw, out, plane, tiles):
        for first, rows in tiles:
            lane = iota((rows, 128), 1)
            low = lane < 64
            take_a = jnp.where(low, 2 * lane, 2 * lane - 127)
            take_b = jnp.where(low, 2 * lane + 1, 2 * lane - 128)
            va = raw[plane, first : first + rows, 0:128]
            vb = raw[plane, first : first + rows, 128:256]
            va = jnp.take_along_axis(va, take_a, axis=1, mode="promise_in_bounds")
            vb = jnp.take_along_axis(vb, take_b, axis=1, mode="promise_in_bounds")
            place = ((plane % 2) * 8 + plane // 2) * 32 + first
            out[0, place : place + rows, :] = jnp.where(low, va, vb)
            out[1, place : place + rows, :] = pltpu.roll(jnp.where(low, vb, va), 64, 1)

    for copy in own:
        copy.wait()
    for x in range(4, 12):
        split(s.raw_u, s.split_u, x, ((8, 16),))
        split(s.raw_f, s.split_f, x, ((8, 16),))
    def split_planes(planes, tiles):
        for x in planes:
            split(s.raw_u, s.split_u, x, tiles)
            if 2 <= x < 13:
                split(s.raw_f, s.split_f, x, tiles)

    def collect(rows, outer):
        for i in rows:
            keep = inside(i - 4, (1, 8, 128), 16)[0]
            for p in range(4):
                at = pl.ds((p % 2) * 256 + i + 4, 8, stride=32)
                u = s.split_u[p // 2, at, :]
                s.u[p, i] = jnp.where(keep, u, 0.0) if outer else u
                if 2 <= i < 22:
                    s.f[p, i] = s.split_f[p // 2, at, :]

    outside_x = (0, 1, 2, 3, 12, 13, 14, 15)
    for copy in round1[12:16]:
        copy.wait_recv()
    split_planes(outside_x, ((8, 16),))
    collect(range(4, 20), False)
    s.u[:, 24:26] = jnp.zeros((4, 2, 8, 128), F32)

    def faces(i, carry):
        at, above = pl.ds(2 * i, 2), pl.ds(2 * i + 1, 2)
        u = [s.u[p, at] for p in range(4)]
        un = [s.u[p, above] for p in range(4)]
        keep = inside(2 * i - 4, (2, 8, 128), 16)
        first = iota((2, 8, 128), 2) == 0
        sx, sz, szd, ky = [], [], [], []
        for z in range(2):
            ka, kb = face(u[2 * z], u[2 * z + 1]), face(u[2 * z + 1], xsh(u[2 * z], 1))
            s.kx[z, at], s.kx[2 + z, at] = ka, kb
            sx.append(0.25 * (ka + kb))
        for x in range(2):
            ka, kb = face(u[x], u[2 + x]), face(u[2 + x], zsh(u[x], 1, 1))
            s.kz[x, at], s.kz[2 + x, at] = ka, kb
            sz.append(0.25 * (ka + kb))
            szd.append(jnp.where(first, face(u[x], 0.0), zsh(sz[x], -1, 1)))
        for p in range(4):
            ky.append(face(u[p], un[p]))
            s.ky[p, at] = ky[p]

        def mx(f0, f1):
            return f0 + 0.25 * (f1 + xsh(f1, -1)), 0.25 * f1

        def mz(f0, f1):
            return f0 + 0.25 * (f1 + zsh(f1, -1, 1)), 0.25 * f1

        sx0, sxp = mz(sx[0], sx[1])
        t0, tp = mx(sz[0], sz[1])
        d0, dp = mx(szd[0], szd[1])
        for k, value in enumerate((sx0, sxp, t0, tp, t0 + d0, tp + dp)):
            s.g[k, at] = jnp.where(keep, value, 0.0)
        h0, hp = mx(ky[0], ky[1])
        j0, jp = mx(ky[2], ky[3])
        h00, h0p = mz(h0, j0)
        hp0, hpp = mz(hp, jp)
        for k, value in enumerate((h00, h0p, hp0, hpp)):
            s.h[k, at] = value
        return carry


    def beside(ref, row, k):
        at = pl.ds(row, k)
        v = [ref[p, at] for p in range(4)]
        out = []
        for z in range(2):
            for x in range(2):
                p = 2 * z + x
                ka, kb = s.kx[z, at], s.kx[2 + z, at]
                w = v[2 * z + 1 - x]
                if x == 0:
                    total = ka * w + xsh(kb * w, -1)
                else:
                    total = ka * w + kb * xsh(w, 1)
                ka, kb = s.kz[x, at], s.kz[2 + x, at]
                w = v[2 * (1 - z) + x]
                if z == 0:
                    total += ka * w + zsh(kb * w, -1, 1)
                else:
                    total += ka * w + kb * zsh(w, 1, 1)
                total += s.ky[p, at] * ref[p, pl.ds(row + 1, k)]
                total += s.ky[p, pl.ds(row - 1, k)] * ref[p, pl.ds(row - 1, k)]
                out.append(total)
        return v, out

    def smooth0(i, carry):
        row = 2 + 2 * i
        at = pl.ds(row, 2)
        keep = inside(row - 4, (2, 8, 128), 16)
        first = iota((2, 8, 128), 2) == 0
        v, total = beside(s.u, row, 2)
        for z in range(2):
            for x in range(2):
                p = 2 * z + x
                ka, kb = s.kx[z, at], s.kx[2 + z, at]
                diag = ka + (xsh(kb, -1) if x == 0 else kb)
                ka, kb = s.kz[x, at], s.kz[2 + x, at]
                if z == 0:
                    diag += ka + jnp.where(first, face(v[p], 0.0), zsh(kb, -1, 1))
                else:
                    diag += ka + kb
                diag += s.ky[p, at] + s.ky[p, pl.ds(row - 1, 2)]
                newton = s.f[p, at] - (diag * v[p] - total[p])
                weight = WEIGHT / diag
                s.f[p, at] = newton
                s.d0[p, at] = diag
                s.w0[p, at] = weight
                s.e0[p, at] = jnp.where(keep, weight * newton, 0.0)
        return carry


    def residual0(i, carry):
        row = 3 + 2 * i
        at = pl.ds(row, 2)
        keep = inside(row - 4, (2, 8, 128), 16)
        v, total = beside(s.e0, row, 2)
        r = [s.f[p, at] - (s.d0[p, at] * v[p] - total[p]) for p in range(4)]
        r = [r[x] + 0.5 * (r[2 + x] + zsh(r[2 + x], -1, 1)) for x in range(2)]
        s.r0[at] = jnp.where(keep, r[0] + 0.5 * (r[1] + xsh(r[1], -1)), 0.0)
        return carry

    def stretch(parts):
        for step, low, high in parts:
            lax.fori_loop(low, high, step, 0, unroll=True)

    stretch(((faces, 2, 9), (smooth0, 2, 8), (residual0, 2, 7)))
    for copy in round1[8:12]:
        copy.wait_recv()
    split_planes(range(4, 12), ((0, 8), (24, 8)))
    for copy in round1[0:8]:
        copy.wait_recv()
    split_planes(outside_x, ((0, 8), (24, 8)))
    collect((0, 1, 2, 3, 20, 21, 22, 23), True)
    stretch(((faces, 0, 2), (faces, 9, 12), (smooth0, 0, 2), (smooth0, 8, 10)))
    stretch(((residual0, 0, 2), (residual0, 7, 9)))

    def level1(i, only_up):
        base = 2 * i
        edge = (gy == 0) & (i == 2)
        keep = inside(i - 2, (1, 8, 128), 8)[0]

        def v_of(q, row):
            return 0.25 * (s.h[q, row] + s.h[q, row + 1])

        v = [v_of(q, base) for q in range(4)]
        up = [0.25 * s.g[k, base + 1] for k in range(6)]
        sx0, sxp, t0, tp, p0, pp = up
        arrays = {
            (0, 0): sx0 + xsh(sx0, -1) + p0 - v[0],
            (0, 1): sxp + xsh(sxp, -1) - t0 - v[1],
            (1, 0): pp - sx0 - v[2],
            (1, 1): -sxp - tp - v[3],
        }
        fill(9, i, arrays, keep)
        if only_up:
            return
        vd = [jnp.where(edge, s.h[q, base - 1], v_of(q, base - 2)) for q in range(4)]
        both = [v[q] + vd[q] for q in range(4)]
        sx0, sxp, t0, tp, p0, pp = [
            s.g[k, base] + up[k] + 0.25 * s.g[k, base - 1] for k in range(6)
        ]
        arrays = {
            (0, 0): sx0 + xsh(sx0, -1) + p0 + both[0],
            (0, 1): sxp + xsh(sxp, -1) - t0 + both[1],
            (1, 0): pp - sx0 + both[2],
            (1, 1): both[3] - sxp - tp,
        }
        fill(0, i, arrays, keep)
        s.w1[i] = jnp.where(keep, WEIGHT / arrays[(0, 0)], 0.0)

    def fill(first, i, arrays, keep):
        for key in arrays:
            arrays[key] = jnp.where(keep, arrays[key], 0.0)
        for a in (-1, 0, 1):
            for c in (-1, 0, 1):
                value = zsh(arrays[(abs(a), abs(c))], min(c, 0), 1)
                s.a1[first + 3 * (a + 1) + c + 1, i] = xsh(value, min(a, 0))

    def coefficient1(o, row, k):
        a, b, c = o
        at = 3 * (a + 1) + c + 1
        if b == 0:
            return s.a1[at, pl.ds(row, k)]
        return s.a1[9 + at, pl.ds(row if b == 1 else row - 1, k)]

    sub = iota((8, 128), 0)

    def start1(y, carry):
        row = 4 + 2 * y
        b1 = s.r0[row] + 0.5 * (s.r0[row - 1] + s.r0[row + 1])
        fine = row

        def mass(k):
            return s.g[k, fine] + 0.25 * (s.g[k, fine + 1] + s.g[k, fine - 1])

        sx0 = mass(0)
        below = 0.25 * (s.h[0, fine - 2] + s.h[0, fine - 1])
        below = jnp.where((gy == 0) & (y == 0), s.h[0, fine - 1], below)
        above = 0.25 * (s.h[0, fine] + s.h[0, fine + 1])
        e1 = WEIGHT * b1 / (sx0 + xsh(sx0, -1) + mass(4) + above + below)
        s.re1[1, y + 2] = jnp.where(sub < 4, pltpu.roll(e1, 6, 0), pltpu.roll(b1, 2, 0))
        return carry

    lax.fori_loop(0, 8, start1, 0, unroll=True)

    mine = {-1: pl.ds(2, 2), 0: pl.ds(2, 8), 1: pl.ds(8, 2)}
    theirs = {-1: pl.ds(10, 2), 0: pl.ds(2, 8), 1: pl.ds(0, 2)}
    round2 = []
    for a, b in AROUND:
        round2.append(send(s.re1.at[1, mine[b]], s.re1.at[1 - a, theirs[b]], number, a, b))
        number += 1

    level1(0, True)

    def level1_step(i, carry):
        level1(i, False)
        return carry

    lax.fori_loop(1, 11, level1_step, 0, unroll=True)

    def coarsen(coefficient, row, d, store):
        def get(o, r):
            return coefficient(o, r, 1)[0]

        y0, y1 = {}, {}
        for a in (-1, 0, 1):
            for c in (-1, 0, 1):
                zero_up = 0.25 * get((a, 0, c), row + 1)
                plus = get((a, 1, c), row)
                y0[a, c] = (
                    get((a, 0, c), row)
                    + zero_up
                    + 0.25 * get((a, 0, c), row - 1)
                    + 0.5
                    * (
                        get((a, -1, c), row)
                        + get((a, -1, c), row + 1)
                        + plus
                        + get((a, 1, c), row - 1)
                    )
                )
                y1[a, c] = 0.5 * (plus + get((a, 1, c), row + 1)) + zero_up

        def three(lo, mid, hi, shift, want):
            out = {}
            q = 0.25 * mid
            lo, hi = 0.5 * lo, 0.5 * hi
            if 0 in want:
                out[0] = mid + lo + hi + shift(q + lo, 1) + shift(q + hi, -1)
            if 1 in want:
                out[1] = hi + shift(q + hi, 1)
            if -1 in want:
                out[-1] = lo + shift(q + lo, -1)
            return out

        def by_z(f, by):
            return zsh(f, by, d)

        for b, table in ((0, y0), (1, y1)):
            xs = {}
            for c in (-1, 0, 1):
                want = (0, 1) if b == 0 else (-1, 0, 1)
                got = three(table[-1, c], table[0, c], table[1, c], xsh, want)
                for a in got:
                    xs[a, c] = got[a]
            for a in (0, 1) if b == 0 else (-1, 0, 1):
                want = (0, 1) if (a, b) == (0, 0) else (-1, 0, 1)
                got = three(xs[a, -1], xs[a, 0], xs[a, 1], by_z, want)
                for c in got:
                    store(FORWARD.index((a, b, c)), got[c])

    def coarsen1(y, carry):
        def store(k, value):
            s.ra2[1, y + 2, k // 4, 2 * (k % 4) : 2 * (k % 4) + 1, :] = value[2:3]
            s.ra2[1, y + 2, k // 4, 2 * (k % 4) + 1 : 2 * (k % 4) + 2, :] = value[4:5]
            if k == 0:
                s.w2own[y] = WEIGHT / value

        coarsen(coefficient1, 2 * y + 2, 1, store)
        return carry

    lax.fori_loop(0, 4, coarsen1, 0, unroll=True)
    mine = {-1: pl.ds(2, 2), 0: pl.ds(2, 4), 1: pl.ds(4, 2)}
    theirs = {-1: pl.ds(6, 2), 0: pl.ds(2, 4), 1: pl.ds(0, 2)}
    round2a = []
    for a, b in AROUND:
        round2a.append(send(s.ra2.at[1, mine[b]], s.ra2.at[1 - a, theirs[b]], number, a, b))
        number += 1
    for b in (-1, 0, 1):
        round2a.append(send(s.ra2.at[1, mine[b], 1], s.ra2.at[3, theirs[b], 1], number, -2, b))
        number += 1

    for copy in round2:
        copy.wait_recv()

    def unpack1(i, carry):
        at = pl.ds(2 * i, 2)
        keep = inside(2 * i - 2, (2, 8, 128), 8)
        sub = iota((2, 8, 128), 1)
        lo, mid, hi = s.re1[0, at], s.re1[1, at], s.re1[2, at]
        e = jnp.where(
            sub < 2,
            pltpu.roll(lo, 6, 1),
            jnp.where(sub < 6, pltpu.roll(mid, 2, 1), pltpu.roll(hi, 6, 1)),
        )
        b = jnp.where(
            sub < 2,
            pltpu.roll(lo, 2, 1),
            jnp.where(sub < 6, pltpu.roll(mid, 6, 1), pltpu.roll(hi, 2, 1)),
        )
        s.e1[at] = jnp.where(keep, e, 0.0)
        s.b1[at] = jnp.where(keep, b, 0.0)
        return carry

    lax.fori_loop(0, 6, unpack1, 0, unroll=True)

    def apply(coefficient, ref, row, k, d):
        total = None
        for b in (-1, 0, 1):
            e = ref[pl.ds(row + b, k)]
            for c in (-1, 0, 1):
                ez = zsh(e, c, d)
                for a in (-1, 0, 1):
                    term = coefficient((a, b, c), row, k) * xsh(ez, a)
                    total = term if total is None else total + term
        return total

    def gather_zx(r, d):
        r = r + 0.5 * (zsh(r, -1, d) + zsh(r, 1, d))
        return r + 0.5 * (xsh(r, -1) + xsh(r, 1))

    def residual1(i, carry):
        row = 1 + i
        keep = inside(row - 2, (1, 8, 128), 8)
        r = s.b1[pl.ds(row, 1)] - apply(coefficient1, s.e1, row, 1, 1)
        s.r1[pl.ds(row, 1)] = jnp.where(keep, gather_zx(r, 1), 0.0)
        return carry

    lax.fori_loop(0, 9, residual1, 0, unroll=True)

    def start2(y, carry):
        row = 2 * y + 2
        b2 = s.r1[row] + 0.5 * (s.r1[row - 1] + s.r1[row + 1])
        e2 = s.w2own[y] * b2
        s.re2[1, y + 2, 0:1, :] = e2[2:3]
        s.re2[1, y + 2, 1:2, :] = e2[4:5]
        s.re2[1, y + 2, 2:3, :] = b2[2:3]
        s.re2[1, y + 2, 3:4, :] = b2[4:5]
        return carry

    lax.fori_loop(0, 4, start2, 0, unroll=True)

    mine = {-1: pl.ds(2, 3), 0: pl.ds(2, 4), 1: pl.ds(4, 2)}
    theirs = {-1: pl.ds(6, 3), 0: pl.ds(2, 4), 1: pl.ds(0, 2)}
    round3 = []
    for a, b in [(-2, -1), (-2, 1)] + AROUND + [(-2, 0)]:
        round3.append(send(s.re2.at[1, mine[b]], s.re2.at[1 - a, theirs[b]], number, a, b))
        number += 1

    for copy in round2a:
        copy.wait_recv()

    def unpack_a2(i, carry):
        at = pl.ds(2 * i, 2)
        keep = inside(2 * i - 2, (2, 8, 128), 4)
        sub = iota((2, 8, 128), 1)
        for t in range(4):
            lo, mid, hi = s.ra2[0, at, t], s.ra2[1, at, t], s.ra2[2, at, t]
            for j in range(4):
                k = 4 * t + j
                if k >= 14:
                    continue

                def rolled(v, to):
                    by = (to - 2 * j) % 8
                    return pltpu.roll(v, by, 1) if by else v

                value = jnp.where(sub < 4, rolled(mid, 2), rolled(hi, 4))
                if t == 1:
                    value = jnp.where(sub < 6, value, rolled(s.ra2[3, at, 1], 6))
                value = jnp.where(sub < 2, rolled(lo, 0), value)
                value = jnp.where(keep, value, 0.0)
                s.a2[k, at] = value
                if k == 0:
                    s.w2[at] = jnp.where(keep, WEIGHT / value, 0.0)
        return carry

    lax.fori_loop(0, 4, unpack_a2, 0, unroll=True)

    def expand(ref, back, row, d):
        for k, (a, b, c) in enumerate(BACKWARD):
            value = ref[FORWARD.index((-a, -b, -c)), pl.ds(row + b, 1)]
            back[k, pl.ds(row, 1)] = xsh(zsh(value, c, d), a)

    def reader(ref, back):
        def coefficient(o, row, k):
            if o in FORWARD:
                return ref[FORWARD.index(o), pl.ds(row, k)]
            return back[BACKWARD.index(o), pl.ds(row, k)]

        return coefficient

    def expand2(i, carry):
        expand(s.a2, s.a2b, i, 2)
        return carry

    lax.fori_loop(1, 8, expand2, 0, unroll=True)
    coefficient2 = reader(s.a2, s.a2b)

    def coarsen2(y, carry):
        def store(k, value):
            s.a3own[k, y] = value

        coarsen(coefficient2, 2 * y + 2, 2, store)
        return carry

    lax.fori_loop(0, 2, coarsen2, 0, unroll=True)
    lane = iota((8, 128), 1)
    middle = pl.ds(24, 8)
    for y in range(2):
        for q in range(4):
            value = s.a3own[4 * q, y]
            for j in range(1, 4):
                if 4 * q + j < 14:
                    other = pltpu.roll(s.a3own[4 * q + j, y], j, 1)
                    value = jnp.where(lane % 4 == j, other, value)
            s.ra3[2, 24 + 4 * y + q : 25 + 4 * y + q, :] = value[2:3]

    def send_wide(ref, number, last=4):
        copies = []
        for a, b in [o for o in WIDE if o[0] <= last]:
            copies.append(send(ref.at[2, middle], ref.at[2 + b, pl.ds(8 * (a + 3), 8)], number, -a, -b))
            number += 1
        return copies, number

    round3a, number = send_wide(s.ra3, number)

    for copy in round3:
        copy.wait_recv()
    for k in range(4):
        at = slice(2 * k, 2 * k + 2)
        keep = inside(-2, (9, 2, 128), 4)
        s.e2[0:9, at, :] = jnp.where(keep, s.re2[k, 0:9, 0:2, :], 0.0)
        s.b2[0:9, at, :] = jnp.where(keep, s.re2[k, 0:9, 2:4, :], 0.0)

    def residual2(i, carry):
        row = 1 + i
        keep = inside(row - 2, (1, 8, 128), 4)
        r = s.b2[pl.ds(row, 1)] - apply(coefficient2, s.e2, row, 1, 2)
        s.r2[pl.ds(row, 1)] = jnp.where(keep, gather_zx(r, 2), 0.0)
        return carry

    lax.fori_loop(0, 5, residual2, 0, unroll=True)
    for y in range(2):
        row = 2 * y + 2
        b3 = s.r2[row] + 0.5 * (s.r2[row - 1] + s.r2[row + 1])
        e3 = WEIGHT * b3 / s.a3own[0, y]
        s.rb3[2, 24 + y : 25 + y, :] = b3[2:3]
        s.rb3[2, 26 + y : 27 + y, :] = e3[2:3]

    round4, number = send_wide(s.rb3, number, 3)
    for copy in round3a:
        copy.wait_recv()

    for dy in range(5):
        for y in range(2):
            row = 2 * dy + y
            keep = inside(row - 4, (1, 8, 128), 2)[0]
            for q in range(4):
                value = jnp.where(keep, s.ra3[dy, pl.ds(4 * y + q, 8, stride=8), :], 0.0)
                for j in range(4):
                    if 4 * q + j < 14:
                        s.a3[4 * q + j, row] = pltpu.roll(value, 128 - j, 1) if j else value
            s.w3[row] = jnp.where(keep, WEIGHT / s.a3[0, row], 0.0)

    def expand3(i, carry):
        expand(s.a3, s.a3b, i, 4)
        return carry

    lax.fori_loop(2, 9, expand3, 0, unroll=True)
    coefficient3 = reader(s.a3, s.a3b)

    for copy in round4:
        copy.wait_recv()
    for dy in range(5):
        for y in range(2):
            row = 2 * dy + y
            keep = inside(row - 4, (1, 8, 128), 2)[0]
            b3 = s.rb3[dy, pl.ds(y, 8, stride=8), :]
            e3 = s.rb3[dy, pl.ds(2 + y, 8, stride=8), :]
            s.b3[row] = jnp.where(keep, b3, 0.0)
            s.e3[0, row] = jnp.where(keep, e3, 0.0)

    def sweep(source, target, low, high):
        def step(row, carry):
            at = pl.ds(row, 1)
            old, new = s.e3.at[source], s.e3.at[target]
            r = s.b3[at] - apply(coefficient3, old, row, 1, 4)
            new[at] = old[at] + s.w3[at] * r
            return carry

        lax.fori_loop(low + 4, high + 5, step, 0, unroll=True)

    sweep(0, 1, -2, 3)
    sweep(1, 0, -1, 2)
    sweep(0, 1, 0, 1)
    for y in range(2):
        s.re3[2, 24 + y : 25 + y, :] = s.e3[1, 4 + y, 3:4, :]

    round5, number = send_wide(s.re3, number)
    for copy in started:
        copy.wait_send()
    for copy in round5:
        copy.wait_recv()
    for dy in range(5):
        for y in range(2):
            row = 2 * dy + y
            keep = inside(row - 4, (1, 8, 128), 2)[0]
            e3 = s.re3[dy, pl.ds(y, 8, stride=8), :]
            s.e3[0, row] = jnp.where(keep, e3, 0.0)
    sweep(0, 1, -2, 4)
    sweep(1, 0, -1, 3)

    def spread(c, first, d, place):
        rows = c.shape[0]
        half = 0.5 * (c + xsh(c, 1))
        for k in range(4):
            place[0:rows, 2 * k : 2 * k + 1, :] = c[:, first + k : first + k + 1]
            place[0:rows, 2 * k + 1 : 2 * k + 2, :] = half[:, first + k : first + k + 1]
        value = place[0:rows]
        coarse = iota(value.shape, 2) % (2 * d) == 0
        place[0:rows] = jnp.where(coarse, value, 0.5 * (zsh(value, -1, d) + zsh(value, 1, d)))

    def add_rows(place, rows, target, width):
        for i in range(rows):
            value = place[i // 2]
            if i % 2:
                value = 0.5 * (value + place[i // 2 + 1])
            keep = inside(i - 2, (1, 8, 128), width)[0]
            target[i] = target[i] + jnp.where(keep, value, 0.0)

    spread(s.e3[0, 3:8], 2, 2, s.place)
    add_rows(s.place, 9, s.e2, 4)

    def post2(row, carry):
        at = pl.ds(row, 1)
        r = s.b2[at] - apply(coefficient2, s.e2, row, 1, 2)
        s.x2[at] = s.e2[at] + s.w2[at] * r
        return carry

    lax.fori_loop(1, 8, post2, 0, unroll=True)
    spread(s.x2[1:8], 1, 1, s.place)
    add_rows(s.place, 12, s.e1, 8)

    def post1(i, carry):
        row = 1 + i
        at = pl.ds(row, 1)
        r = s.b1[at] - apply(coefficient1, s.e1, row, 1, 1)
        s.x1[at] = s.e1[at] + s.w1[at] * r
        return carry

    lax.fori_loop(0, 10, post1, 0, unroll=True)
    s.x1[11] = jnp.zeros((8, 128), F32)

    def prolong0(i, carry):
        c = s.x1[i]
        for step in range(2):
            row = 2 * i + step
            keep = inside(row - 4, (1, 8, 128), 16)[0]
            if step:
                c = 0.5 * (c + s.x1[i + 1])
            cz = 0.5 * (c + zsh(c, 1, 1))
            values = (c, 0.5 * (c + xsh(c, 1)), cz, 0.5 * (cz + xsh(cz, 1)))
            for p in range(4):
                s.e0[p, row] = s.e0[p, row] + jnp.where(keep, values[p], 0.0)
        return carry

    lax.fori_loop(1, 11, prolong0, 0, unroll=True)

    def finish(i, carry):
        row = 4 + 2 * i
        at = pl.ds(row, 2)
        v, total = beside(s.e0, row, 2)
        sub = iota((2, 8, 128), 1)
        for z in range(2):
            done = []
            for x in range(2):
                p = 2 * z + x
                r = s.f[p, at] - (s.d0[p, at] * v[p] - total[p])
                value = s.u[p, at] + (v[p] + s.w0[p, at] * r)
                done.append(pltpu.roll(value, 6 if x == 0 else 2, 1))
            both = jnp.where(sub < 4, done[0], done[1])
            for k in range(2):
                s.co[z, pl.ds(pl.multiple_of(16 * i + 8 * k, 8), 8), :] = both[k]
        return carry

    lax.fori_loop(0, 8, finish, 0, unroll=True)

    lane = iota((16, 128), 1)
    low = lane < 64
    take = jnp.where(lane % 2 == 0, lane // 2, 64 + lane // 2)
    for x in range(8):
        place = (x % 2) * 4 + x // 2
        even = s.co[0, pl.ds(place, 16, stride=8), :]
        odd = pltpu.roll(s.co[1, pl.ds(place, 16, stride=8), :], 64, 1)
        va, vb = jnp.where(low, even, odd), pltpu.roll(jnp.where(low, odd, even), 64, 1)
        o_ref[x, :, 0:128] = jnp.take_along_axis(va, take, axis=1, mode="promise_in_bounds")
        o_ref[x, :, 128:256] = jnp.take_along_axis(vb, take, axis=1, mode="promise_in_bounds")


COPIES = 16 + 8 + 11 + 11 + 3 * len(WIDE)
TILE = (8, 128)
SHAPES = {
    "raw_u": (16, 32, 256),
    "raw_f": (16, 32, 256),
    "split_u": (2, 512, 128),
    "split_f": (2, 512, 128),
    "co": (2, 128, 128),
    "u": (4, 26) + TILE,
    "f": (4, 26) + TILE,
    "kx": (4, 24) + TILE,
    "kz": (4, 24) + TILE,
    "ky": (4, 24) + TILE,
    "g": (6, 24) + TILE,
    "h": (4, 24) + TILE,
    "d0": (4, 24) + TILE,
    "w0": (4, 24) + TILE,
    "e0": (4, 26) + TILE,
    "r0": (24,) + TILE,
    "a1": (18, 12) + TILE,
    "w1": (12,) + TILE,
    "re1": (3, 12) + TILE,
    "e1": (12,) + TILE,
    "b1": (12,) + TILE,
    "x1": (12,) + TILE,
    "r1": (12,) + TILE,
    "ra2": (4, 8, 4) + TILE,
    "w2own": (4,) + TILE,
    "a2": (14, 8) + TILE,
    "a2b": (13, 8) + TILE,
    "w2": (8,) + TILE,
    "re2": (4, 9) + TILE,
    "e2": (9,) + TILE,
    "b2": (9,) + TILE,
    "x2": (9,) + TILE,
    "r2": (9,) + TILE,
    "a3own": (14, 2) + TILE,
    "ra3": (5, 64, 128),
    "rb3": (5, 64, 128),
    "re3": (5, 64, 128),
    "a3": (14, 10) + TILE,
    "a3b": (13, 10) + TILE,
    "w3": (10,) + TILE,
    "b3": (10,) + TILE,
    "e3": (2, 10) + TILE,
    "place": (8,) + TILE,
}


class Scratch:
    pass


def on_device(n, m, state, forcing):
    names = list(SHAPES)

    def body(x_ref, f_ref, o_ref, *scratch):
        s = Scratch()
        for name, ref in zip(names, scratch):
            setattr(s, name, ref)
        s.ssem, s.rsem, s.lsem = scratch[len(names) :]
        kernel_body(n, m, x_ref, f_ref, o_ref, s)

    return pl.pallas_call(
        body,
        out_shape=jax.ShapeDtypeStruct(state.shape, F32),
        in_specs=[pl.BlockSpec(memory_space=pl.ANY)] * 2,
        out_specs=pl.BlockSpec(memory_space=pltpu.VMEM),
        scratch_shapes=[pltpu.VMEM(shape, F32) for shape in SHAPES.values()]
        + [pltpu.SemaphoreType.DMA((COPIES,))] * 2
        + [pltpu.SemaphoreType.DMA((2,))],
        compiler_params=pltpu.CompilerParams(
            collective_id=0, has_side_effects=True, vmem_limit_bytes=48 << 20
        ),
    )(*[pltpu.with_memory_space_constraint(v, pltpu.HBM) for v in (state, forcing)])


def solution(mesh):
    n, m = mesh.shape["gx"], mesh.shape["gy"]
    return jax.shard_map(
        lambda state, forcing: on_device(n, m, state, forcing),
        mesh=mesh,
        in_specs=(P("gx", "gy", None), P("gx", "gy", None)),
        out_specs=P("gx", "gy", None),
        check_vma=False,
    )
```

```python
import jax
import jax.numpy as jnp
from jax import lax
from jax.experimental import pallas as pl
from jax.experimental.pallas import tpu as pltpu
from jax.sharding import PartitionSpec as P

WEIGHT = 0.6
MESH = pl.DeviceIdType.MESH
F32 = jnp.float32

AROUND = [(-1, -1), (-1, 1), (1, -1), (1, 1), (0, -1), (0, 1), (-1, 0), (1, 0)]
GREETED = AROUND + [(2, 0)]
WIDE = sorted(
    [(a, b) for a in range(-3, 5) for b in range(-2, 3) if (a, b) != (0, 0)],
    key=lambda o: -(abs(o[0]) + 2 * abs(o[1])),
)
FORWARD = [(0, 0, 0), (0, 0, 1), (1, 0, -1), (1, 0, 0), (1, 0, 1)] + [
    (a, 1, c) for a in (-1, 0, 1) for c in (-1, 0, 1)
]
ALL = [(a, b, c) for b in (-1, 0, 1) for a in (-1, 0, 1) for c in (-1, 0, 1)]
BACKWARD = [o for o in ALL if o not in FORWARD]


def iota(shape, dim):
    return lax.broadcasted_iota(jnp.int32, shape, dim)


def xsh(f, by):
    if by == 0:
        return f
    return pltpu.roll(f, 7 if by == 1 else 1, f.ndim - 2)


def zsh(f, by, d):
    if by == 0:
        return f
    lane = iota(f.shape, f.ndim - 1)
    if by == 1:
        return jnp.where(lane < 128 - d, pltpu.roll(f, 128 - d, f.ndim - 1), 0.0)
    return jnp.where(lane >= d, pltpu.roll(f, d, f.ndim - 1), 0.0)


def face(a, b):
    return 1.0 + jnp.square(0.5 * (a + b))


def kernel_body(n, m, x_ref, f_ref, o_ref, s):
    gx, gy = lax.axis_index("gx"), lax.axis_index("gy")

    def device(a, b):
        return (lax.rem(gx + a + n, n), lax.rem(gy + b + m, m))

    started = []

    def send(src, dst, number, a, b):
        copy = pltpu.make_async_remote_copy(
            src_ref=src,
            dst_ref=dst,
            send_sem=s.ssem.at[number],
            recv_sem=s.rsem.at[number],
            device_id=device(a, b),
            device_id_type=MESH,
        )
        copy.start()
        started.append(copy)
        return copy

    def inside(first, shape, width):
        rows = gy * width + first + iota(shape, 0)
        return (rows >= 0) & (rows < m * width)

    barrier = pltpu.get_barrier_semaphore()
    for a, b in GREETED:
        pl.semaphore_signal(barrier, inc=1, device_id=device(a, b), device_id_type=MESH)

    here_x = {-1: pl.ds(0, 4), 0: pl.ds(0, 8), 1: pl.ds(4, 4)}
    there_x = {-1: pl.ds(12, 4), 0: pl.ds(4, 8), 1: pl.ds(0, 4)}
    here_y = {-1: pl.ds(0, 4), 0: pl.ds(0, 16), 1: pl.ds(12, 4)}
    there_y = {-1: pl.ds(24, 4), 0: pl.ds(8, 16), 1: pl.ds(4, 4)}
    here_fx = {-1: pl.ds(0, 1), 0: pl.ds(0, 8), 1: pl.ds(6, 2)}
    there_fx = {-1: pl.ds(12, 1), 0: pl.ds(4, 8), 1: pl.ds(2, 2)}
    own = [
        pltpu.make_async_copy(ref, raw.at[4:12, 8:24], s.lsem.at[k])
        for k, (ref, raw) in enumerate(((x_ref, s.raw_u), (f_ref, s.raw_f)))
    ]
    for copy in own:
        copy.start()
    pl.semaphore_wait(barrier, len(GREETED))
    round1 = []
    number = 0
    for a, b in AROUND:
        for ref, raw, hx, tx in (
            (x_ref, s.raw_u, here_x, there_x),
            (f_ref, s.raw_f, here_fx, there_fx),
        ):
            round1.append(
                send(ref.at[hx[a], here_y[b]], raw.at[tx[a], there_y[b]], number, a, b)
            )
            number += 1

    def split(raw, out, plane, tiles):
        for first, rows in tiles:
            lane = iota((rows, 128), 1)
            low = lane < 64
            take_a = jnp.where(low, 2 * lane, 2 * lane - 127)
            take_b = jnp.where(low, 2 * lane + 1, 2 * lane - 128)
            va = raw[plane, first : first + rows, 0:128]
            vb = raw[plane, first : first + rows, 128:256]
            va = jnp.take_along_axis(va, take_a, axis=1, mode="promise_in_bounds")
            vb = jnp.take_along_axis(vb, take_b, axis=1, mode="promise_in_bounds")
            place = ((plane % 2) * 8 + plane // 2) * 32 + first
            out[0, place : place + rows, :] = jnp.where(low, va, vb)
            out[1, place : place + rows, :] = pltpu.roll(jnp.where(low, vb, va), 64, 1)

    for copy in own:
        copy.wait()
    for x in range(4, 12):
        split(s.raw_u, s.split_u, x, ((8, 16),))
        split(s.raw_f, s.split_f, x, ((8, 16),))
    def split_planes(planes, tiles):
        for x in planes:
            split(s.raw_u, s.split_u, x, tiles)
            if 2 <= x < 13:
                split(s.raw_f, s.split_f, x, tiles)

    def collect(rows, outer):
        for i in rows:
            keep = inside(i - 4, (1, 8, 128), 16)[0]
            for p in range(4):
                at = pl.ds((p % 2) * 256 + i + 4, 8, stride=32)
                u = s.split_u[p // 2, at, :]
                s.u[p, i] = jnp.where(keep, u, 0.0) if outer else u
                if 2 <= i < 22:
                    s.f[p, i] = s.split_f[p // 2, at, :]

    outside_x = (0, 1, 2, 3, 12, 13, 14, 15)
    for copy in round1[12:16]:
        copy.wait_recv()
    split_planes(outside_x, ((8, 16),))
    collect(range(4, 20), False)
    s.u[:, 24:26] = jnp.zeros((4, 2, 8, 128), F32)

    def faces(i, carry):
        at, above = pl.ds(2 * i, 2), pl.ds(2 * i + 1, 2)
        u = [s.u[p, at] for p in range(4)]
        un = [s.u[p, above] for p in range(4)]
        keep = inside(2 * i - 4, (2, 8, 128), 16)
        first = iota((2, 8, 128), 2) == 0
        sx, sz, szd, ky = [], [], [], []
        for z in range(2):
            ka, kb = face(u[2 * z], u[2 * z + 1]), face(u[2 * z + 1], xsh(u[2 * z], 1))
            s.kx[z, at], s.kx[2 + z, at] = ka, kb
            sx.append(0.25 * (ka + kb))
        for x in range(2):
            ka, kb = face(u[x], u[2 + x]), face(u[2 + x], zsh(u[x], 1, 1))
            s.kz[x, at], s.kz[2 + x, at] = ka, kb
            sz.append(0.25 * (ka + kb))
            szd.append(jnp.where(first, face(u[x], 0.0), zsh(sz[x], -1, 1)))
        for p in range(4):
            ky.append(face(u[p], un[p]))
            s.ky[p, at] = ky[p]

        def mx(f0, f1):
            return f0 + 0.25 * (f1 + xsh(f1, -1)), 0.25 * f1

        def mz(f0, f1):
            return f0 + 0.25 * (f1 + zsh(f1, -1, 1)), 0.25 * f1

        sx0, sxp = mz(sx[0], sx[1])
        t0, tp = mx(sz[0], sz[1])
        d0, dp = mx(szd[0], szd[1])
        for k, value in enumerate((sx0, sxp, t0, tp, t0 + d0, tp + dp)):
            s.g[k, at] = jnp.where(keep, value, 0.0)
        h0, hp = mx(ky[0], ky[1])
        j0, jp = mx(ky[2], ky[3])
        h00, h0p = mz(h0, j0)
        hp0, hpp = mz(hp, jp)
        for k, value in enumerate((h00, h0p, hp0, hpp)):
            s.h[k, at] = value
        return carry


    def beside(ref, row, k):
        at = pl.ds(row, k)
        v = [ref[p, at] for p in range(4)]
        out = []
        for z in range(2):
            for x in range(2):
                p = 2 * z + x
                ka, kb = s.kx[z, at], s.kx[2 + z, at]
                w = v[2 * z + 1 - x]
                if x == 0:
                    total = ka * w + xsh(kb * w, -1)
                else:
                    total = ka * w + kb * xsh(w, 1)
                ka, kb = s.kz[x, at], s.kz[2 + x, at]
                w = v[2 * (1 - z) + x]
                if z == 0:
                    total += ka * w + zsh(kb * w, -1, 1)
                else:
                    total += ka * w + kb * zsh(w, 1, 1)
                total += s.ky[p, at] * ref[p, pl.ds(row + 1, k)]
                total += s.ky[p, pl.ds(row - 1, k)] * ref[p, pl.ds(row - 1, k)]
                out.append(total)
        return v, out

    def smooth0(i, carry):
        row = 2 + 2 * i
        at = pl.ds(row, 2)
        keep = inside(row - 4, (2, 8, 128), 16)
        first = iota((2, 8, 128), 2) == 0
        v, total = beside(s.u, row, 2)
        for z in range(2):
            for x in range(2):
                p = 2 * z + x
                ka, kb = s.kx[z, at], s.kx[2 + z, at]
                diag = ka + (xsh(kb, -1) if x == 0 else kb)
                ka, kb = s.kz[x, at], s.kz[2 + x, at]
                if z == 0:
                    diag += ka + jnp.where(first, face(v[p], 0.0), zsh(kb, -1, 1))
                else:
                    diag += ka + kb
                diag += s.ky[p, at] + s.ky[p, pl.ds(row - 1, 2)]
                newton = s.f[p, at] - (diag * v[p] - total[p])
                weight = WEIGHT / diag
                s.f[p, at] = newton
                s.d0[p, at] = diag
                s.w0[p, at] = weight
                s.e0[p, at] = jnp.where(keep, weight * newton, 0.0)
        return carry


    def residual0(i, carry):
        row = 3 + 2 * i
        at = pl.ds(row, 2)
        keep = inside(row - 4, (2, 8, 128), 16)
        v, total = beside(s.e0, row, 2)
        r = [s.f[p, at] - (s.d0[p, at] * v[p] - total[p]) for p in range(4)]
        r = [r[x] + 0.5 * (r[2 + x] + zsh(r[2 + x], -1, 1)) for x in range(2)]
        s.r0[at] = jnp.where(keep, r[0] + 0.5 * (r[1] + xsh(r[1], -1)), 0.0)
        return carry

    def stretch(parts):
        for step, low, high in parts:
            lax.fori_loop(low, high, step, 0, unroll=True)

    stretch(((faces, 2, 9), (smooth0, 2, 8), (residual0, 2, 7)))
    for copy in round1[8:12]:
        copy.wait_recv()
    split_planes(range(4, 12), ((0, 8), (24, 8)))
    for copy in round1[0:8]:
        copy.wait_recv()
    split_planes(outside_x, ((0, 8), (24, 8)))
    collect((0, 1, 2, 3, 20, 21, 22, 23), True)
    stretch(((faces, 0, 2), (faces, 9, 12), (smooth0, 0, 2), (smooth0, 8, 10)))
    stretch(((residual0, 0, 2), (residual0, 7, 9)))

    def level1(i, only_up):
        base = 2 * i
        edge = (gy == 0) & (i == 2)
        keep = inside(i - 2, (1, 8, 128), 8)[0]

        def v_of(q, row):
            return 0.25 * (s.h[q, row] + s.h[q, row + 1])

        v = [v_of(q, base) for q in range(4)]
        up = [0.25 * s.g[k, base + 1] for k in range(6)]
        sx0, sxp, t0, tp, p0, pp = up
        arrays = {
            (0, 0): sx0 + xsh(sx0, -1) + p0 - v[0],
            (0, 1): sxp + xsh(sxp, -1) - t0 - v[1],
            (1, 0): pp - sx0 - v[2],
            (1, 1): -sxp - tp - v[3],
        }
        fill(9, i, arrays, keep)
        if only_up:
            return
        vd = [jnp.where(edge, s.h[q, base - 1], v_of(q, base - 2)) for q in range(4)]
        both = [v[q] + vd[q] for q in range(4)]
        sx0, sxp, t0, tp, p0, pp = [
            s.g[k, base] + up[k] + 0.25 * s.g[k, base - 1] for k in range(6)
        ]
        arrays = {
            (0, 0): sx0 + xsh(sx0, -1) + p0 + both[0],
            (0, 1): sxp + xsh(sxp, -1) - t0 + both[1],
            (1, 0): pp - sx0 + both[2],
            (1, 1): both[3] - sxp - tp,
        }
        fill(0, i, arrays, keep)
        s.w1[i] = jnp.where(keep, WEIGHT / arrays[(0, 0)], 0.0)

    def fill(first, i, arrays, keep):
        for key in arrays:
            arrays[key] = jnp.where(keep, arrays[key], 0.0)
        for a in (-1, 0, 1):
            for c in (-1, 0, 1):
                value = zsh(arrays[(abs(a), abs(c))], min(c, 0), 1)
                s.a1[first + 3 * (a + 1) + c + 1, i] = xsh(value, min(a, 0))

    def coefficient1(o, row, k):
        a, b, c = o
        at = 3 * (a + 1) + c + 1
        if b == 0:
            return s.a1[at, pl.ds(row, k)]
        return s.a1[9 + at, pl.ds(row if b == 1 else row - 1, k)]

    sub = iota((8, 128), 0)

    def start1(y, carry):
        row = 4 + 2 * y
        b1 = s.r0[row] + 0.5 * (s.r0[row - 1] + s.r0[row + 1])
        fine = row

        def mass(k):
            return s.g[k, fine] + 0.25 * (s.g[k, fine + 1] + s.g[k, fine - 1])

        sx0 = mass(0)
        below = 0.25 * (s.h[0, fine - 2] + s.h[0, fine - 1])
        below = jnp.where((gy == 0) & (y == 0), s.h[0, fine - 1], below)
        above = 0.25 * (s.h[0, fine] + s.h[0, fine + 1])
        e1 = WEIGHT * b1 / (sx0 + xsh(sx0, -1) + mass(4) + above + below)
        s.re1[1, y + 2] = jnp.where(sub < 4, pltpu.roll(e1, 6, 0), pltpu.roll(b1, 2, 0))
        return carry

    lax.fori_loop(0, 8, start1, 0, unroll=True)

    mine = {-1: pl.ds(2, 2), 0: pl.ds(2, 8), 1: pl.ds(8, 2)}
    theirs = {-1: pl.ds(10, 2), 0: pl.ds(2, 8), 1: pl.ds(0, 2)}
    round2 = []
    for a, b in AROUND:
        round2.append(send(s.re1.at[1, mine[b]], s.re1.at[1 - a, theirs[b]], number, a, b))
        number += 1

    level1(0, True)

    def level1_step(i, carry):
        level1(i, False)
        return carry

    lax.fori_loop(1, 11, level1_step, 0, unroll=True)

    def coarsen(coefficient, row, d, store):
        def get(o, r):
            return coefficient(o, r, 1)[0]

        y0, y1 = {}, {}
        for a in (-1, 0, 1):
            for c in (-1, 0, 1):
                zero_up = 0.25 * get((a, 0, c), row + 1)
                plus = get((a, 1, c), row)
                y0[a, c] = (
                    get((a, 0, c), row)
                    + zero_up
                    + 0.25 * get((a, 0, c), row - 1)
                    + 0.5
                    * (
                        get((a, -1, c), row)
                        + get((a, -1, c), row + 1)
                        + plus
                        + get((a, 1, c), row - 1)
                    )
                )
                y1[a, c] = 0.5 * (plus + get((a, 1, c), row + 1)) + zero_up

        def three(lo, mid, hi, shift, want):
            out = {}
            q = 0.25 * mid
            lo, hi = 0.5 * lo, 0.5 * hi
            if 0 in want:
                out[0] = mid + lo + hi + shift(q + lo, 1) + shift(q + hi, -1)
            if 1 in want:
                out[1] = hi + shift(q + hi, 1)
            if -1 in want:
                out[-1] = lo + shift(q + lo, -1)
            return out

        def by_z(f, by):
            return zsh(f, by, d)

        for b, table in ((0, y0), (1, y1)):
            xs = {}
            for c in (-1, 0, 1):
                want = (0, 1) if b == 0 else (-1, 0, 1)
                got = three(table[-1, c], table[0, c], table[1, c], xsh, want)
                for a in got:
                    xs[a, c] = got[a]
            for a in (0, 1) if b == 0 else (-1, 0, 1):
                want = (0, 1) if (a, b) == (0, 0) else (-1, 0, 1)
                got = three(xs[a, -1], xs[a, 0], xs[a, 1], by_z, want)
                for c in got:
                    store(FORWARD.index((a, b, c)), got[c])

    def coarsen1(y, carry):
        def store(k, value):
            s.ra2[1, y + 2, k // 4, 2 * (k % 4) : 2 * (k % 4) + 1, :] = value[2:3]
            s.ra2[1, y + 2, k // 4, 2 * (k % 4) + 1 : 2 * (k % 4) + 2, :] = value[4:5]
            if k == 0:
                s.w2own[y] = WEIGHT / value

        coarsen(coefficient1, 2 * y + 2, 1, store)
        return carry

    lax.fori_loop(0, 4, coarsen1, 0, unroll=True)
    mine = {-1: pl.ds(2, 2), 0: pl.ds(2, 4), 1: pl.ds(4, 2)}
    theirs = {-1: pl.ds(6, 2), 0: pl.ds(2, 4), 1: pl.ds(0, 2)}
    round2a = []
    for a, b in AROUND:
        round2a.append(send(s.ra2.at[1, mine[b]], s.ra2.at[1 - a, theirs[b]], number, a, b))
        number += 1
    for b in (-1, 0, 1):
        round2a.append(send(s.ra2.at[1, mine[b], 1], s.ra2.at[3, theirs[b], 1], number, -2, b))
        number += 1

    for copy in round2:
        copy.wait_recv()

    def unpack1(i, carry):
        at = pl.ds(2 * i, 2)
        keep = inside(2 * i - 2, (2, 8, 128), 8)
        sub = iota((2, 8, 128), 1)
        lo, mid, hi = s.re1[0, at], s.re1[1, at], s.re1[2, at]
        e = jnp.where(
            sub < 2,
            pltpu.roll(lo, 6, 1),
            jnp.where(sub < 6, pltpu.roll(mid, 2, 1), pltpu.roll(hi, 6, 1)),
        )
        b = jnp.where(
            sub < 2,
            pltpu.roll(lo, 2, 1),
            jnp.where(sub < 6, pltpu.roll(mid, 6, 1), pltpu.roll(hi, 2, 1)),
        )
        s.e1[at] = jnp.where(keep, e, 0.0)
        s.b1[at] = jnp.where(keep, b, 0.0)
        return carry

    lax.fori_loop(0, 6, unpack1, 0, unroll=True)

    def apply(coefficient, ref, row, k, d):
        total = None
        for b in (-1, 0, 1):
            e = ref[pl.ds(row + b, k)]
            for c in (-1, 0, 1):
                ez = zsh(e, c, d)
                for a in (-1, 0, 1):
                    term = coefficient((a, b, c), row, k) * xsh(ez, a)
                    total = term if total is None else total + term
        return total

    def gather_zx(r, d):
        r = r + 0.5 * (zsh(r, -1, d) + zsh(r, 1, d))
        return r + 0.5 * (xsh(r, -1) + xsh(r, 1))

    def residual1(i, carry):
        row = 1 + i
        keep = inside(row - 2, (1, 8, 128), 8)
        r = s.b1[pl.ds(row, 1)] - apply(coefficient1, s.e1, row, 1, 1)
        s.r1[pl.ds(row, 1)] = jnp.where(keep, gather_zx(r, 1), 0.0)
        return carry

    lax.fori_loop(0, 9, residual1, 0, unroll=True)

    def start2(y, carry):
        row = 2 * y + 2
        b2 = s.r1[row] + 0.5 * (s.r1[row - 1] + s.r1[row + 1])
        e2 = s.w2own[y] * b2
        s.re2[1, y + 2, 0:1, :] = e2[2:3]
        s.re2[1, y + 2, 1:2, :] = e2[4:5]
        s.re2[1, y + 2, 2:3, :] = b2[2:3]
        s.re2[1, y + 2, 3:4, :] = b2[4:5]
        return carry

    lax.fori_loop(0, 4, start2, 0, unroll=True)

    mine = {-1: pl.ds(2, 3), 0: pl.ds(2, 4), 1: pl.ds(4, 2)}
    theirs = {-1: pl.ds(6, 3), 0: pl.ds(2, 4), 1: pl.ds(0, 2)}
    round3 = []
    for a, b in [(-2, -1), (-2, 1)] + AROUND + [(-2, 0)]:
        round3.append(send(s.re2.at[1, mine[b]], s.re2.at[1 - a, theirs[b]], number, a, b))
        number += 1

    for copy in round2a:
        copy.wait_recv()

    def unpack_a2(i, carry):
        at = pl.ds(2 * i, 2)
        keep = inside(2 * i - 2, (2, 8, 128), 4)
        sub = iota((2, 8, 128), 1)
        for t in range(4):
            lo, mid, hi = s.ra2[0, at, t], s.ra2[1, at, t], s.ra2[2, at, t]
            for j in range(4):
                k = 4 * t + j
                if k >= 14:
                    continue

                def rolled(v, to):
                    by = (to - 2 * j) % 8
                    return pltpu.roll(v, by, 1) if by else v

                value = jnp.where(sub < 4, rolled(mid, 2), rolled(hi, 4))
                if t == 1:
                    value = jnp.where(sub < 6, value, rolled(s.ra2[3, at, 1], 6))
                value = jnp.where(sub < 2, rolled(lo, 0), value)
                value = jnp.where(keep, value, 0.0)
                s.a2[k, at] = value
                if k == 0:
                    s.w2[at] = jnp.where(keep, WEIGHT / value, 0.0)
        return carry

    lax.fori_loop(0, 4, unpack_a2, 0, unroll=True)

    def expand(ref, back, row, d):
        for k, (a, b, c) in enumerate(BACKWARD):
            value = ref[FORWARD.index((-a, -b, -c)), pl.ds(row + b, 1)]
            back[k, pl.ds(row, 1)] = xsh(zsh(value, c, d), a)

    def reader(ref, back):
        def coefficient(o, row, k):
            if o in FORWARD:
                return ref[FORWARD.index(o), pl.ds(row, k)]
            return back[BACKWARD.index(o), pl.ds(row, k)]

        return coefficient

    def expand2(i, carry):
        expand(s.a2, s.a2b, i, 2)
        return carry

    lax.fori_loop(1, 8, expand2, 0, unroll=True)
    coefficient2 = reader(s.a2, s.a2b)

    def coarsen2(y, carry):
        def store(k, value):
            s.a3own[k, y] = value

        coarsen(coefficient2, 2 * y + 2, 2, store)
        return carry

    lax.fori_loop(0, 2, coarsen2, 0, unroll=True)
    lane = iota((8, 128), 1)
    for y in range(2):
        for q in range(4):
            value = s.a3own[4 * q, y]
            for j in range(1, 4):
                if 4 * q + j < 14:
                    other = pltpu.roll(s.a3own[4 * q + j, y], j, 1)
                    value = jnp.where(lane % 4 == j, other, value)
            s.ra3[2, 24 + 4 * y + q : 25 + 4 * y + q, :] = value[2:3]

    def send_wide(ref, number, last, rows):
        copies = []
        for a, b in [o for o in WIDE if o[0] <= last]:
            copies.append(send(ref.at[2, pl.ds(24, rows)], ref.at[2 + b, pl.ds(8 * (a + 3), rows)], number, -a, -b))
            number += 1
        return copies, number

    round3a, number = send_wide(s.ra3, number, 4, 8)

    for copy in round3:
        copy.wait_recv()
    for k in range(4):
        at = slice(2 * k, 2 * k + 2)
        keep = inside(-2, (9, 2, 128), 4)
        s.e2[0:9, at, :] = jnp.where(keep, s.re2[k, 0:9, 0:2, :], 0.0)
        s.b2[0:9, at, :] = jnp.where(keep, s.re2[k, 0:9, 2:4, :], 0.0)

    def residual2(i, carry):
        row = 1 + i
        keep = inside(row - 2, (1, 8, 128), 4)
        r = s.b2[pl.ds(row, 1)] - apply(coefficient2, s.e2, row, 1, 2)
        s.r2[pl.ds(row, 1)] = jnp.where(keep, gather_zx(r, 2), 0.0)
        return carry

    lax.fori_loop(0, 5, residual2, 0, unroll=True)
    for y in range(2):
        row = 2 * y + 2
        b3 = s.r2[row] + 0.5 * (s.r2[row - 1] + s.r2[row + 1])
        e3 = WEIGHT * b3 / s.a3own[0, y]
        s.rb3[2, 24 + y : 25 + y, :] = b3[2:3]
        s.rb3[2, 26 + y : 27 + y, :] = e3[2:3]

    round4, number = send_wide(s.rb3, number, 3, 4)
    for copy in round3a:
        copy.wait_recv()

    for dy in range(5):
        for y in range(2):
            row = 2 * dy + y
            keep = inside(row - 4, (1, 8, 128), 2)[0]
            for q in range(4):
                value = jnp.where(keep, s.ra3[dy, pl.ds(4 * y + q, 8, stride=8), :], 0.0)
                for j in range(4):
                    if 4 * q + j < 14:
                        s.a3[4 * q + j, row] = pltpu.roll(value, 128 - j, 1) if j else value
            s.w3[row] = jnp.where(keep, WEIGHT / s.a3[0, row], 0.0)

    def expand3(i, carry):
        expand(s.a3, s.a3b, i, 4)
        return carry

    lax.fori_loop(2, 9, expand3, 0, unroll=True)
    coefficient3 = reader(s.a3, s.a3b)

    for copy in round4:
        copy.wait_recv()
    for dy in range(5):
        for y in range(2):
            row = 2 * dy + y
            keep = inside(row - 4, (1, 8, 128), 2)[0]
            b3 = s.rb3[dy, pl.ds(y, 8, stride=8), :]
            e3 = s.rb3[dy, pl.ds(2 + y, 8, stride=8), :]
            s.b3[row] = jnp.where(keep, b3, 0.0)
            s.e3[0, row] = jnp.where(keep, e3, 0.0)

    def sweep(source, target, low, high):
        def step(row, carry):
            at = pl.ds(row, 1)
            old, new = s.e3.at[source], s.e3.at[target]
            r = s.b3[at] - apply(coefficient3, old, row, 1, 4)
            new[at] = old[at] + s.w3[at] * r
            return carry

        lax.fori_loop(low + 4, high + 5, step, 0, unroll=True)

    sweep(0, 1, -2, 3)
    sweep(1, 0, -1, 2)
    sweep(0, 1, 0, 1)
    for y in range(2):
        s.re3[2, 24 + y : 25 + y, :] = s.e3[1, 4 + y, 3:4, :]

    round5, number = send_wide(s.re3, number, 4, 2)
    for copy in started:
        copy.wait_send()
    for copy in round5:
        copy.wait_recv()
    for dy in range(5):
        for y in range(2):
            row = 2 * dy + y
            keep = inside(row - 4, (1, 8, 128), 2)[0]
            e3 = s.re3[dy, pl.ds(y, 8, stride=8), :]
            s.e3[0, row] = jnp.where(keep, e3, 0.0)
    sweep(0, 1, -2, 4)
    sweep(1, 0, -1, 3)

    def spread(c, first, d, place):
        rows = c.shape[0]
        half = 0.5 * (c + xsh(c, 1))
        for k in range(4):
            place[0:rows, 2 * k : 2 * k + 1, :] = c[:, first + k : first + k + 1]
            place[0:rows, 2 * k + 1 : 2 * k + 2, :] = half[:, first + k : first + k + 1]
        value = place[0:rows]
        coarse = iota(value.shape, 2) % (2 * d) == 0
        place[0:rows] = jnp.where(coarse, value, 0.5 * (zsh(value, -1, d) + zsh(value, 1, d)))

    def add_rows(place, rows, target, width):
        for i in range(rows):
            value = place[i // 2]
            if i % 2:
                value = 0.5 * (value + place[i // 2 + 1])
            keep = inside(i - 2, (1, 8, 128), width)[0]
            target[i] = target[i] + jnp.where(keep, value, 0.0)

    spread(s.e3[0, 3:8], 2, 2, s.place)
    add_rows(s.place, 9, s.e2, 4)

    def post2(row, carry):
        at = pl.ds(row, 1)
        r = s.b2[at] - apply(coefficient2, s.e2, row, 1, 2)
        s.x2[at] = s.e2[at] + s.w2[at] * r
        return carry

    lax.fori_loop(1, 8, post2, 0, unroll=True)
    spread(s.x2[1:8], 1, 1, s.place)
    add_rows(s.place, 12, s.e1, 8)

    def post1(i, carry):
        row = 1 + i
        at = pl.ds(row, 1)
        r = s.b1[at] - apply(coefficient1, s.e1, row, 1, 1)
        s.x1[at] = s.e1[at] + s.w1[at] * r
        return carry

    lax.fori_loop(0, 10, post1, 0, unroll=True)
    s.x1[11] = jnp.zeros((8, 128), F32)

    def prolong0(i, carry):
        c = s.x1[i]
        for step in range(2):
            row = 2 * i + step
            keep = inside(row - 4, (1, 8, 128), 16)[0]
            if step:
                c = 0.5 * (c + s.x1[i + 1])
            cz = 0.5 * (c + zsh(c, 1, 1))
            values = (c, 0.5 * (c + xsh(c, 1)), cz, 0.5 * (cz + xsh(cz, 1)))
            for p in range(4):
                s.e0[p, row] = s.e0[p, row] + jnp.where(keep, values[p], 0.0)
        return carry

    lax.fori_loop(1, 11, prolong0, 0, unroll=True)

    def finish(i, carry):
        row = 4 + 2 * i
        at = pl.ds(row, 2)
        v, total = beside(s.e0, row, 2)
        sub = iota((2, 8, 128), 1)
        for z in range(2):
            done = []
            for x in range(2):
                p = 2 * z + x
                r = s.f[p, at] - (s.d0[p, at] * v[p] - total[p])
                value = s.u[p, at] + (v[p] + s.w0[p, at] * r)
                done.append(pltpu.roll(value, 6 if x == 0 else 2, 1))
            both = jnp.where(sub < 4, done[0], done[1])
            for k in range(2):
                s.co[z, pl.ds(pl.multiple_of(16 * i + 8 * k, 8), 8), :] = both[k]
        return carry

    lax.fori_loop(0, 8, finish, 0, unroll=True)

    lane = iota((16, 128), 1)
    low = lane < 64
    take = jnp.where(lane % 2 == 0, lane // 2, 64 + lane // 2)
    for x in range(8):
        place = (x % 2) * 4 + x // 2
        even = s.co[0, pl.ds(place, 16, stride=8), :]
        odd = pltpu.roll(s.co[1, pl.ds(place, 16, stride=8), :], 64, 1)
        va, vb = jnp.where(low, even, odd), pltpu.roll(jnp.where(low, odd, even), 64, 1)
        o_ref[x, :, 0:128] = jnp.take_along_axis(va, take, axis=1, mode="promise_in_bounds")
        o_ref[x, :, 128:256] = jnp.take_along_axis(vb, take, axis=1, mode="promise_in_bounds")


COPIES = 16 + 8 + 11 + 11 + 3 * len(WIDE)
TILE = (8, 128)
SHAPES = {
    "raw_u": (16, 32, 256),
    "raw_f": (16, 32, 256),
    "split_u": (2, 512, 128),
    "split_f": (2, 512, 128),
    "co": (2, 128, 128),
    "u": (4, 26) + TILE,
    "f": (4, 26) + TILE,
    "kx": (4, 24) + TILE,
    "kz": (4, 24) + TILE,
    "ky": (4, 24) + TILE,
    "g": (6, 24) + TILE,
    "h": (4, 24) + TILE,
    "d0": (4, 24) + TILE,
    "w0": (4, 24) + TILE,
    "e0": (4, 26) + TILE,
    "r0": (24,) + TILE,
    "a1": (18, 12) + TILE,
    "w1": (12,) + TILE,
    "re1": (3, 12) + TILE,
    "e1": (12,) + TILE,
    "b1": (12,) + TILE,
    "x1": (12,) + TILE,
    "r1": (12,) + TILE,
    "ra2": (4, 8, 4) + TILE,
    "w2own": (4,) + TILE,
    "a2": (14, 8) + TILE,
    "a2b": (13, 8) + TILE,
    "w2": (8,) + TILE,
    "re2": (4, 9) + TILE,
    "e2": (9,) + TILE,
    "b2": (9,) + TILE,
    "x2": (9,) + TILE,
    "r2": (9,) + TILE,
    "a3own": (14, 2) + TILE,
    "ra3": (5, 64, 128),
    "rb3": (5, 64, 128),
    "re3": (5, 64, 128),
    "a3": (14, 10) + TILE,
    "a3b": (13, 10) + TILE,
    "w3": (10,) + TILE,
    "b3": (10,) + TILE,
    "e3": (2, 10) + TILE,
    "place": (8,) + TILE,
}


class Scratch:
    pass


def on_device(n, m, state, forcing):
    names = list(SHAPES)

    def body(x_ref, f_ref, o_ref, *scratch):
        s = Scratch()
        for name, ref in zip(names, scratch):
            setattr(s, name, ref)
        s.ssem, s.rsem, s.lsem = scratch[len(names) :]
        kernel_body(n, m, x_ref, f_ref, o_ref, s)

    return pl.pallas_call(
        body,
        out_shape=jax.ShapeDtypeStruct(state.shape, F32),
        in_specs=[pl.BlockSpec(memory_space=pl.ANY)] * 2,
        out_specs=pl.BlockSpec(memory_space=pltpu.VMEM),
        scratch_shapes=[pltpu.VMEM(shape, F32) for shape in SHAPES.values()]
        + [pltpu.SemaphoreType.DMA((COPIES,))] * 2
        + [pltpu.SemaphoreType.DMA((2,))],
        compiler_params=pltpu.CompilerParams(
            collective_id=0, has_side_effects=True, vmem_limit_bytes=48 << 20
        ),
    )(*[pltpu.with_memory_space_constraint(v, pltpu.HBM) for v in (state, forcing)])


def solution(mesh):
    n, m = mesh.shape["gx"], mesh.shape["gy"]
    return jax.shard_map(
        lambda state, forcing: on_device(n, m, state, forcing),
        mesh=mesh,
        in_specs=(P("gx", "gy", None), P("gx", "gy", None)),
        out_specs=P("gx", "gy", None),
        check_vma=False,
    )
```
